32 devices in a mesh: groups: 2 (over x), seq: 16 (over z, y, core).
Axes of the slice: x: 2, y: 2, z: 4, core: 2. Of those that a mesh axis runs over, the one named last changes fastest.
Arguments:
- tokens: bfloat16 [1024, 512, 512], P(('groups', 'seq')), parts along dimension 0, may hold values from -6 to 6
- cotangent: bfloat16 [1024, 512, 512], P('groups', 'seq'), parts along dimension 0, may hold values from -6 to 6
- w_first: bfloat16 [512, 512], P('seq'), may hold values from -0.25 to 0.25
- w_second: bfloat16 [512, 512], P('seq'), may hold values from -0.25 to 0.25
- mask_first: int32 [4, 4], replicated, may hold values from 0 to 1, as said below
- mask_second: int32 [4, 4], replicated, may hold values from 0 to 1, as said below
- gate_values: bfloat16 [1024, 512], P(('groups', 'seq')), parts along dimension 0, may hold values from -4 to 4
Outputs:
- grad_tokens: bfloat16 [1024, 512, 512], P(('groups', 'seq')), parts along dimension 0
- grad_first: float32 [1024, 512], P(('groups', 'seq')), parts along dimension 0
- grad_second: float32 [1024, 512], P(('groups', 'seq')), parts along dimension 0
The draws below stay inside these ranges and needn't reach their ends.
There are 2 independent parts, one for each index of `groups`. The reference program is written for one: setup_inputs(seed, part) draws one part's arguments, and reference() takes and returns one part's arrays. A program takes and returns all parts, laid end to end along the dimension named above; an argument that names none is the same for every part. Nothing has to cross between parts.
Inputs may be any that keep to these rules, and one draw needn't show every extreme that they name: `mask_first`: the diagonal blocks of each factor are always kept. `mask_second`: the diagonal blocks of each factor are always kept.
All inputs are finite; a program needn't handle non-finite values.
Results may differ from the reference program's by a relative error of at most 0.0054.
Values may be sent and summed in bfloat16 or wider, within the bound.
A program may use at most 320 MiB of HBM per device.

```python
import math
import jax
import jax.numpy as jnp

S = 512
C = 512
BLK = 128
NB = 4


def block_mask(key):
    chosen = jax.random.randint(key, (NB, NB), 0, 2)
    labels = jnp.arange(NB, dtype=jnp.int32)
    diagonal = labels[:, None] == labels[None, :]
    return jnp.where(diagonal, 1, chosen).astype(jnp.int32)


def draw_mask_first(key, part):
    return block_mask(jax.random.fold_in(key, 11))


def draw_mask_second(key, part):
    return block_mask(jax.random.fold_in(key, 23))


def raised(values, stream_key, source, target, blocks, factor):
    def block_of(axis_at):
        return (jnp.arange(values.shape[axis_at]) // (values.shape[axis_at] // blocks)).reshape((-1,) + (1,) * (values.ndim - 1 - axis_at))

    near = jax.random.permutation(stream_key, blocks)[block_of(target)]
    other_side = (block_of(target) + blocks // 2) % blocks
    return jnp.where((block_of(source) == near) | (block_of(source) == other_side), factor * values, values)


def level_of(stream_key, extent, cuts, least, largest):
    level = 1.0
    for axis_at, shards_of in cuts:
        steps = jax.random.uniform(jax.random.fold_in(jax.random.fold_in(stream_key, 6), axis_at), (shards_of,), jnp.float32, least / len(cuts), largest / len(cuts))
        level = level * jnp.repeat(jnp.exp(steps), extent[axis_at] // shards_of).reshape((-1,) + (1,) * (len(extent) - 1 - axis_at))
    return level


def bell_draw(own_key, shape, width, limit, cuts=(), kind=jnp.bfloat16):
    entries = width * jax.random.normal(own_key, shape, jnp.float32)
    if cuts:
        entries = entries * level_of(own_key, shape, cuts, -0.22, 0.18)
    return jnp.clip(entries, -limit, limit).astype(kind)


def noise_with(own_key, extent, scale, reach, shards, heavy, kind=jnp.bfloat16):
    drawn = scale * jax.random.normal(own_key, extent, jnp.float32)
    if shards:
        drawn = drawn * level_of(own_key, extent, shards, -0.22, 0.18)
    return jnp.clip(raised(drawn, jax.random.fold_in(own_key, 3), *heavy), -reach, reach).astype(kind)


def setup_inputs(seed: int = 0, part: int = 0) -> dict:
    arg_keys = jax.random.split(jax.random.key(seed), 8)
    part_splits = jax.random.split(jax.random.fold_in(arg_keys[7], part), 8)
    return {
        "tokens": noise_with(part_splits[0], (S, S, C), 1.0, 6.0, ((0, 16),), (0, 1, 16, 2.0)),
        "cotangent": noise_with(part_splits[1], (S, S, C), 1.0, 6.0, ((1, 16),), (1, 0, 16, 2.0)),
        "w_first": bell_draw(arg_keys[2], (S, S), S ** -0.5, 0.25, ((0, 16),)),
        "w_second": bell_draw(arg_keys[3], (S, S), S ** -0.5, 0.25, ((0, 16),)),
        "mask_first": draw_mask_first(jax.random.fold_in(arg_keys[7], 71), part),
        "mask_second": draw_mask_second(jax.random.fold_in(arg_keys[7], 71), part),
        "gate_values": bell_draw(part_splits[6], (S, S), 1.0, 4.0, ((0, 16),)),
    }


def expand_mask(mask):
    blocks = (jnp.arange(S, dtype=jnp.int32) // BLK).astype(jnp.int32)
    return mask[blocks][:, blocks].astype(jnp.float32)

def reference(tokens, cotangent, w_first, w_second, mask_first, mask_second, gate_values):
    keep_first = expand_mask(mask_first)
    keep_second = expand_mask(mask_second)
    w1m = (w_first.astype(jnp.float32) * keep_first).astype(jnp.bfloat16).astype(jnp.float32)
    w2m = (w_second.astype(jnp.float32) * keep_second).astype(jnp.bfloat16).astype(jnp.float32)
    gate_full = gate_values.astype(jnp.float32)
    x_full = tokens.astype(jnp.float32)
    gated = x_full * gate_full[:, :, None]
    hidden = jnp.einsum('ijc,kj->ikc', x_full, w1m)
    mixed = (hidden * gated).astype(jnp.bfloat16).astype(jnp.float32)
    cot_full = cotangent.astype(jnp.float32)
    back_mixed = jnp.einsum('ki,kjc->ijc', w2m, cot_full).astype(jnp.bfloat16).astype(jnp.float32)
    raw_second = jnp.einsum('kjc,ijc->ki', cot_full, mixed)
    back_hidden = (back_mixed * gated).astype(jnp.bfloat16).astype(jnp.float32)
    direct = gate_full[:, :, None] * back_mixed * hidden
    through = jnp.einsum('ikc,kj->ijc', back_hidden, w1m)
    grad_tokens = (direct + through).astype(jnp.bfloat16)
    raw_first = jnp.einsum('ikc,ijc->kj', back_hidden, x_full)
    factor = 1.0 / math.sqrt(S * C)
    grad_first = keep_first * raw_first * factor
    grad_second = keep_second * raw_second * factor
    return (grad_tokens, grad_first, grad_second)
```

```python
import functools
import math

import jax
import jax.numpy as jnp
from jax import lax
from jax.experimental import pallas as pl
from jax.experimental.pallas import tpu as pltpu
from jax.sharding import PartitionSpec as P

BLK = 128
PLANE = 4
CHUNKS = 8
AHEAD = 4
ORDER = (8, 1, 4, 9, 2, 12, 10, 3, 5, 11, 6, 13, 14, 7, 15)
MESH = pl.DeviceIdType.MESH
F32 = jnp.float32
BF16 = jnp.bfloat16


def flip(x, d):
    y = x
    for b in range(d.bit_length()):
        if (d >> b) & 1:
            y = y + (1 << b) - lax.rem(lax.div(x, 1 << b), 2) * (2 << b)
    return y


def drain(ref, sem):
    pltpu.make_async_copy(ref, ref, sem).wait()


def dot(a, b):
    return lax.dot_general(a, b, (((1,), (0,)), ((), ())), preferred_element_type=F32)


def dot_t(a, b):
    return lax.dot_general(a, b, (((1,), (1,)), ((), ())), preferred_element_type=F32)


def mixer_kernel(
    n, tok, cot, w1, w2, mask1, mask2, gate,
    gt_out, g1_out, g2_out, mix_send, mix_recv, back_send, back_recv,
    full1, full2, w1m, w1t, w2t, gate_t, cot_t, stage, tall, tok_in, back_in, out_stage, hidden_b,
    raw1, raw1_in, raw1_plane, raw1_last, raw2, raw2_in, raw2_plane, raw2_last,
    gather_s, gather_r, mix_s, mix_r, back_s, back_r, load_sem, stage_sem, out_sem, back_sem,
    sum1_s, sum1_r, sum2_s, sum2_r,
):
    rows, extent, channels = tok.shape
    planes = n // PLANE
    h = rows // CHUNKS
    wide = n * h
    me = lax.axis_index("seq")
    z, l = lax.div(me, PLANE), lax.rem(me, PLANE)
    factor = 1.0 / math.sqrt(extent * channels)
    lane_chunks = channels // 128
    half_c = min(256, channels)

    def device(q):
        return {"seq": q}

    def load_tok(c, slot):
        return pltpu.make_async_copy(tok.at[pl.ds(c * h, h)], tok_in.at[slot], load_sem.at[slot])

    def load_cot(c, slot):
        return pltpu.make_async_copy(cot.at[pl.ds(c * wide, wide)], stage.at[slot], stage_sem.at[slot])

    load_tok(0, 0).start()
    load_cot(0, 0).start()

    barrier = pltpu.get_barrier_semaphore()
    for d in range(1, n):
        pl.semaphore_signal(barrier, 1, device_id=device(flip(me, d)), device_id_type=MESH)
    pl.semaphore_wait(barrier, n - 1)

    for a, (w, full) in enumerate(((w1, full1), (w2, full2))):
        for d in range(1, planes):
            pltpu.make_async_remote_copy(
                w, full.at[pl.ds(me * rows, rows)], gather_s.at[a, 0], gather_r.at[a, 0],
                device_id=device(flip(z, d) * PLANE + l), device_id_type=MESH,
            ).start()
    full1[pl.ds(me * rows, rows)] = w1[...]
    full2[pl.ds(me * rows, rows)] = w2[...]

    def spread(a, full):
        drain(full.at[pl.ds(0, (planes - 1) * rows)], gather_r.at[a, 0])
        for d in range(1, PLANE):
            for zz in range(planes):
                part = full.at[pl.ds((zz * PLANE + l) * rows, rows)]
                pltpu.make_async_remote_copy(
                    part, part, gather_s.at[a, 1], gather_r.at[a, 1],
                    device_id=device(z * PLANE + flip(l, d)), device_id_type=MESH,
                ).start()

    def gathered(a, full):
        drain(full.at[pl.ds(0, planes * (PLANE - 1) * rows)], gather_r.at[a, 1])

    def masked(full, mask, plain, turned):
        for i in range(extent // BLK):
            for j in range(extent // BLK):
                block = full[i * BLK:(i + 1) * BLK, j * BLK:(j + 1) * BLK].astype(F32)
                block = block * mask[i, j].astype(F32)
                if plain is not None:
                    plain[i * BLK:(i + 1) * BLK, j * BLK:(j + 1) * BLK] = block.astype(BF16)
                turned[j * BLK:(j + 1) * BLK, i * BLK:(i + 1) * BLK] = block.T.astype(BF16)

    gate_t[...] = gate[...].astype(F32).T

    def gate_column(i):
        lanes = lax.broadcasted_iota(jnp.int32, (extent, rows), 1)
        return jnp.sum(jnp.where(lanes == i, gate_t[...], 0.0), axis=1, keepdims=True)

    spread(0, full1)
    spread(1, full2)
    gathered(0, full1)
    masked(full1, mask1, w1m, w1t)

    def mix_start(c):
        for d in ORDER:
            q = flip(me, d)
            pltpu.make_async_remote_copy(
                mix_send.at[pl.ds(c * h, h), pl.ds(q * rows, rows), :],
                mix_recv.at[c, pl.ds(me * h, h)],
                mix_s.at[c], mix_r.at[c], device_id=device(q), device_id_type=MESH,
            ).start()
        pltpu.make_async_copy(
            mix_send.at[pl.ds(c * h, h), pl.ds(me * rows, rows), :],
            mix_recv.at[c, pl.ds(me * h, h)], mix_r.at[c],
        ).start()

    def mix_chunk(c, carry):
        slot = lax.rem(c, 2)
        load_tok(c, slot).wait()

        @pl.when(c + 1 < CHUNKS)
        def _():
            load_tok(c + 1, 1 - slot).start()

        def row(t, carry):
            g = gate_column(c * h + t)
            for b in range(channels // half_c):
                cs = pl.ds(b * half_c, half_c)
                x = tok_in[slot, t, :, cs]
                hidden = dot(w1m[...], x)
                out_stage[slot, t, :, cs] = (hidden * (x.astype(F32) * g)).astype(BF16)
            return carry

        lax.fori_loop(0, h, row, 0)
        copy = pltpu.make_async_copy(out_stage.at[slot], mix_send.at[pl.ds(c * h, h)], out_sem.at[slot])
        copy.start()
        copy.wait()

        @pl.when(c < AHEAD)
        def _():
            mix_start(c)

        return carry

    lax.fori_loop(0, CHUNKS, mix_chunk, 0)

    gathered(1, full2)
    masked(full2, mask2, None, w2t)
    cot_chunks = extent // wide

    def turn_chunk(c, carry):
        slot = lax.rem(c, 2)
        load_cot(c, slot).wait()

        @pl.when(c + 1 < cot_chunks)
        def _():
            load_cot(c + 1, 1 - slot).start()

        for b in range(lane_chunks):
            cs = pl.ds(b * 128, 128)
            cot_t[:, pl.ds(c * wide, wide), cs] = jnp.swapaxes(stage[slot, :, :, cs], 0, 1)
        return carry

    lax.fori_loop(0, cot_chunks, turn_chunk, 0)

    def back_store(b, s):
        return pltpu.make_async_copy(
            stage.at[s], back_send.at[pl.ds(b * 2 * wide + s * wide, wide)], stage_sem.at[s]
        )

    def back_block(b, carry):
        def column(j, carry):
            tall[j] = dot(w2t[pl.ds(b * 2 * wide, 2 * wide), :], cot_t[j]).astype(BF16)
            return carry

        lax.fori_loop(0, rows, column, 0)
        for s in range(2):
            @pl.when(b > 0)
            def _():
                back_store(b - 1, s).wait()

            for e in range(lane_chunks):
                cs = pl.ds(e * 128, 128)
                stage[s, :, :, cs] = jnp.swapaxes(tall[:, s * wide:(s + 1) * wide, cs], 0, 1)
            back_store(b, s).start()
        return carry

    blocks = extent // (2 * wide)
    lax.fori_loop(0, blocks, back_block, 0)
    for s in range(2):
        back_store(blocks - 1, s).wait()

    def back_start(c, carry):
        for d in ORDER:
            q = flip(me, d)
            pltpu.make_async_remote_copy(
                back_send.at[pl.ds(q * rows + c * h, h)],
                back_recv.at[pl.ds(c * h, h), pl.ds(me * rows, rows), :],
                back_s.at[c], back_r.at[c], device_id=device(q), device_id_type=MESH,
            ).start()
        pltpu.make_async_copy(
            back_send.at[pl.ds(me * rows + c * h, h)],
            back_recv.at[pl.ds(c * h, h), pl.ds(me * rows, rows), :], back_r.at[c],
        ).start()
        return carry

    lax.fori_loop(0, CHUNKS, back_start, 0)

    def mix_late(c, carry):
        mix_start(c)
        return carry

    lax.fori_loop(AHEAD, CHUNKS, mix_late, 0)

    def second(m):
        for s in range(2):
            drain(mix_recv.at[2 * m + s], mix_r.at[2 * m + s])
            copy = pltpu.make_async_copy(mix_recv.at[2 * m + s], stage.at[s], stage_sem.at[s])
            copy.start()
            copy.wait()
            for e in range(lane_chunks):
                cs = pl.ds(e * 128, 128)
                tall[:, s * wide:(s + 1) * wide, cs] = jnp.swapaxes(stage[s, :, :, cs], 0, 1)
        raw2[m] = jnp.zeros(raw2.shape[1:], F32)

        def columns(j, carry):
            part = dot_t(cot_t[4 * j], tall[4 * j])
            for u in range(1, 4):
                part = part + dot_t(cot_t[4 * j + u], tall[4 * j + u])
            raw2[m] += part.reshape(raw2.shape[1:])
            return carry

        lax.fori_loop(0, rows // 4, columns, 0)

    def plane_start(k, src, dst):
        for d in range(1, PLANE):
            other = flip(l, d)
            pltpu.make_async_remote_copy(
                src.at[:, other], dst.at[l], sum1_s.at[k], sum1_r.at[k],
                device_id=device(z * PLANE + other), device_id_type=MESH,
            ).start()

    def plane_sum(k, src, dst, total, last):
        drain(dst.at[pl.ds(0, PLANE - 1)], sum1_r.at[k])
        value = src[:, l]
        for d in range(1, PLANE):
            value = value + dst[flip(l, d)]
        total[...] = value
        for d in range(1, planes):
            other = flip(z, d)
            pltpu.make_async_remote_copy(
                total.at[other], last.at[z], sum2_s.at[k], sum2_r.at[k],
                device_id=device(other * PLANE + l), device_id_type=MESH,
            ).start()

    def whole_sum(k, total, last):
        drain(last.at[pl.ds(0, planes - 1)], sum2_r.at[k])
        value = total[z]
        for d in range(1, planes):
            value = value + last[flip(z, d)]
        return value

    parts = CHUNKS // 2
    early = AHEAD // 2
    for m in range(early):
        second(m)
        plane_start(m, raw2.at[m], raw2_in.at[m])

    raw1[...] = jnp.zeros(raw1.shape, F32)

    def store_rows(c, slot):
        return pltpu.make_async_copy(out_stage.at[slot], gt_out.at[pl.ds(c * h, h)], out_sem.at[slot])

    def rows_chunk(c, carry):
        slot = lax.rem(c, 2)
        load_tok(c, slot).start()
        drain(back_recv.at[pl.ds(c * h, h)], back_r.at[c])
        copy = pltpu.make_async_copy(back_recv.at[pl.ds(c * h, h)], back_in, back_sem)
        copy.start()
        load_tok(c, slot).wait()
        copy.wait()

        @pl.when(c >= 2)
        def _():
            store_rows(c - 2, slot).wait()

        def row(t, carry):
            g = gate_column(c * h + t)
            for b in range(channels // half_c):
                cs = pl.ds(b * half_c, half_c)
                x = tok_in[slot, t, :, cs]
                back = back_in[t, :, cs].astype(F32)
                hidden_b[:, cs] = (back * (x.astype(F32) * g)).astype(BF16)
                hidden = dot(w1m[...], x)
                through = dot(w1t[...], hidden_b[:, cs])
                out_stage[slot, t, :, cs] = (g * back * hidden + through).astype(BF16)
            raw1[...] += dot_t(hidden_b[...], tok_in[slot, t]).reshape(raw1.shape)
            return carry

        lax.fori_loop(0, h, row, 0)
        store_rows(c, slot).start()
        return carry

    lax.fori_loop(0, CHUNKS, rows_chunk, 0)
    k1 = parts
    plane_start(k1, raw1, raw1_in)
    for m in range(early):
        plane_sum(m, raw2.at[m], raw2_in.at[m], raw2_plane.at[m], raw2_last.at[m])
    for m in range(early, parts):
        second(m)
        plane_start(m, raw2.at[m], raw2_in.at[m])
        if m == early:
            plane_sum(k1, raw1, raw1_in, raw1_plane, raw1_last)
        if m < parts - 1:
            plane_sum(m, raw2.at[m], raw2_in.at[m], raw2_plane.at[m], raw2_last.at[m])
        else:
            store_rows(CHUNKS - 2, CHUNKS % 2).wait()
            store_rows(CHUNKS - 1, (CHUNKS - 1) % 2).wait()
            plane_sum(m, raw2.at[m], raw2_in.at[m], raw2_plane.at[m], raw2_last.at[m])

    owner = lax.div(me * rows, BLK)
    first = whole_sum(k1, raw1_plane, raw1_last)
    for j in range(extent // BLK):
        js = slice(j * BLK, (j + 1) * BLK)
        g1_out[:, js] = mask1[owner, j].astype(F32) * first[:, js] * factor

    lane = lax.broadcasted_iota(jnp.int32, (2 * wide, extent), 0)
    target = lax.broadcasted_iota(jnp.int32, (2 * wide, extent), 1)
    result = jnp.zeros((rows, extent), F32)
    for m in range(parts):
        piece = lax.div(lane, wide)
        source = lax.div(lane - piece * wide, h)
        index = source * rows + (2 * m + piece) * h + lax.rem(lane, h)
        pick = (index == target).astype(F32)
        value = whole_sum(m, raw2_plane.at[m], raw2_last.at[m])
        result = result + lax.dot_general(
            value, pick, (((1,), (0,)), ((), ())),
            precision=lax.Precision.HIGHEST, preferred_element_type=F32,
        )
    for j in range(extent // BLK):
        js = slice(j * BLK, (j + 1) * BLK)
        g2_out[:, js] = mask2[owner, j].astype(F32) * result[:, js] * factor

    for a, full in enumerate((full1, full2)):
        drain(full.at[pl.ds(0, (planes - 1) * rows)], gather_s.at[a, 0])
        drain(full.at[pl.ds(0, planes * (PLANE - 1) * rows)], gather_s.at[a, 1])

    def sent(c, carry):
        drain(mix_recv.at[c, pl.ds(0, (n - 1) * h)], mix_s.at[c])
        drain(mix_recv.at[c, pl.ds(0, (n - 1) * h)], back_s.at[c])
        return carry

    lax.fori_loop(0, CHUNKS, sent, 0)
    for m in range(parts):
        drain(raw2_in.at[m, pl.ds(0, PLANE - 1)], sum1_s.at[m])
        drain(raw2_last.at[m, pl.ds(0, planes - 1)], sum2_s.at[m])
    drain(raw1_in.at[pl.ds(0, PLANE - 1)], sum1_s.at[k1])
    drain(raw1_last.at[pl.ds(0, planes - 1)], sum2_s.at[k1])


def fused(n, tokens, cotangent, w_first, w_second, mask_first, mask_second, gate_values):
    rows, extent, channels = tokens.shape
    planes = n // PLANE
    h = rows // CHUNKS
    wide = n * h
    parts = CHUNKS // 2
    hbm = pl.BlockSpec(memory_space=pltpu.HBM)
    vmem = pl.BlockSpec(memory_space=pltpu.VMEM)
    smem = pl.BlockSpec(memory_space=pltpu.SMEM)
    square = pltpu.VMEM((extent, extent), BF16)
    outs = pl.pallas_call(
        functools.partial(mixer_kernel, n),
        out_shape=[
            jax.ShapeDtypeStruct(tokens.shape, BF16),
            jax.ShapeDtypeStruct((rows, extent), F32),
            jax.ShapeDtypeStruct((rows, extent), F32),
            jax.ShapeDtypeStruct((rows, extent, channels), BF16),
            jax.ShapeDtypeStruct((CHUNKS, wide, rows, channels), BF16),
            jax.ShapeDtypeStruct((extent, rows, channels), BF16),
            jax.ShapeDtypeStruct((rows, extent, channels), BF16),
        ],
        in_specs=[hbm, hbm, vmem, vmem, smem, smem, vmem],
        out_specs=[hbm, vmem, vmem, hbm, hbm, hbm, hbm],
        scratch_shapes=[
            square, square, square, square, square,
            pltpu.VMEM((extent, rows), F32),
            pltpu.VMEM((rows, extent, channels), BF16),
            pltpu.VMEM((2, wide, rows, channels), BF16),
            pltpu.VMEM((rows, 2 * wide, channels), BF16),
            pltpu.VMEM((2, h, extent, channels), BF16),
            pltpu.VMEM((h, extent, channels), BF16),
            pltpu.VMEM((2, h, extent, channels), BF16),
            pltpu.VMEM((extent, channels), BF16),
            pltpu.VMEM((planes, PLANE, rows, extent), F32),
            pltpu.VMEM((PLANE, planes, rows, extent), F32),
            pltpu.VMEM((planes, rows, extent), F32),
            pltpu.VMEM((planes, rows, extent), F32),
            pltpu.VMEM((parts, planes, PLANE, rows, 2 * wide), F32),
            pltpu.VMEM((parts, PLANE, planes, rows, 2 * wide), F32),
            pltpu.VMEM((parts, planes, rows, 2 * wide), F32),
            pltpu.VMEM((parts, planes, rows, 2 * wide), F32),
            pltpu.SemaphoreType.DMA((2, 2)),
            pltpu.SemaphoreType.DMA((2, 2)),
            pltpu.SemaphoreType.DMA((CHUNKS,)),
            pltpu.SemaphoreType.DMA((CHUNKS,)),
            pltpu.SemaphoreType.DMA((CHUNKS,)),
            pltpu.SemaphoreType.DMA((CHUNKS,)),
            pltpu.SemaphoreType.DMA((2,)),
            pltpu.SemaphoreType.DMA((2,)),
            pltpu.SemaphoreType.DMA((2,)),
            pltpu.SemaphoreType.DMA,
            pltpu.SemaphoreType.DMA((parts + 1,)),
            pltpu.SemaphoreType.DMA((parts + 1,)),
            pltpu.SemaphoreType.DMA((parts + 1,)),
            pltpu.SemaphoreType.DMA((parts + 1,)),
        ],
        compiler_params=pltpu.CompilerParams(
            collective_id=0, has_side_effects=True, vmem_limit_bytes=60 * 2**20
        ),
        cost_estimate=pl.CostEstimate(
            flops=12 * rows * extent * extent * channels,
            bytes_accessed=20 * rows * extent * channels,
            transcendentals=0,
        ),
        name="mixer_backward",
    )(tokens, cotangent, w_first, w_second, mask_first, mask_second, gate_values)
    return tuple(outs[:3])


def expand_rows(mask, row_ids, extent):
    labels = jnp.arange(mask.shape[0], dtype=jnp.int32)
    row_pick = ((row_ids // BLK)[:, None] == labels[None, :]).astype(jnp.float32)
    col_pick = ((jnp.arange(extent, dtype=jnp.int32) // BLK)[:, None] == labels[None, :]).astype(
        jnp.float32
    )
    return jnp.dot(jnp.dot(row_pick, mask.astype(jnp.float32)), col_pick.T)


def plain(tokens, cotangent, w_first, w_second, mask_first, mask_second, gate_values):
    position = lax.axis_index("seq")
    extent = tokens.shape[1]
    channels = tokens.shape[2]
    shard_rows = w_first.shape[0]
    row_ids = position * shard_rows + jnp.arange(shard_rows, dtype=jnp.int32)
    keep_first = expand_rows(mask_first, row_ids, extent)
    keep_second = expand_rows(mask_second, row_ids, extent)
    local_first = (w_first.astype(jnp.float32) * keep_first).astype(jnp.bfloat16)
    local_second = (w_second.astype(jnp.float32) * keep_second).astype(jnp.bfloat16)
    full = lax.all_gather(jnp.stack([local_first, local_second]), "seq", axis=1, tiled=True)
    full_first, full_second = full[0], full[1]
    shards = extent // shard_rows
    rows = tokens.shape[0]
    cols = cotangent.shape[1]
    flat_cot = lax.optimization_barrier(cotangent.reshape(extent, cols * channels))
    back_flat = lax.dot_general(
        full_second, flat_cot, (((0,), (0,)), ((), ())), preferred_element_type=jnp.float32
    ).astype(jnp.bfloat16)
    back_send = lax.optimization_barrier(back_flat.reshape(shards, rows, cols * channels))
    back_recv = lax.all_to_all(back_send, "seq", split_axis=0, concat_axis=0, tiled=True)
    tokens_late, back_send = lax.optimization_barrier((tokens, back_send))
    gate_full = gate_values.astype(jnp.float32)[:, :, None]
    gated = tokens_late.astype(jnp.float32) * gate_full
    hidden = jnp.einsum("ijc,kj->ikc", tokens_late, full_first, preferred_element_type=jnp.float32)
    mixed = (hidden * gated).astype(jnp.bfloat16)
    mixed_send = mixed.reshape(rows, shards, cols * channels).transpose(1, 0, 2)
    mixed_send, back_recv = lax.optimization_barrier((mixed_send, back_recv))
    flat_cols = lax.all_to_all(mixed_send, "seq", split_axis=0, concat_axis=0, tiled=True)
    back_rows = (
        back_recv.reshape(shards, rows, cols, channels).transpose(1, 0, 2, 3).reshape(tokens.shape)
    )
    back_float = back_rows.astype(jnp.float32)
    back_hidden = (back_float * gated).astype(jnp.bfloat16)
    direct = gate_full * back_float * hidden
    through = jnp.einsum("ikc,kj->ijc", back_hidden, full_first, preferred_element_type=jnp.float32)
    grad_tokens = (direct + through).astype(jnp.bfloat16)
    part_first = jnp.einsum(
        "ikc,ijc->kj", back_hidden, tokens_late, preferred_element_type=jnp.float32
    )
    summed_first = lax.psum_scatter(part_first, "seq", scatter_dimension=0, tiled=True)
    flat_cols, grad_tokens, summed_first = lax.optimization_barrier(
        (flat_cols, grad_tokens, summed_first)
    )
    part_second = lax.dot_general(
        flat_cot,
        flat_cols.reshape(extent, cols * channels),
        (((1,), (1,)), ((), ())),
        preferred_element_type=jnp.float32,
    )
    spread = lax.all_to_all(
        part_second.reshape(shards, shard_rows, extent), "seq", split_axis=0, concat_axis=0, tiled=True
    )
    summed_second = jnp.sum(spread, axis=0)
    factor = 1.0 / math.sqrt(extent * channels)
    grad_first = keep_first * summed_first * factor
    grad_second = keep_second * summed_second * factor
    return (grad_tokens, grad_first, grad_second)


def per_device(n, tokens, cotangent, w_first, w_second, mask_first, mask_second, gate_values):
    if n == 16 and tokens.shape[0] % (4 * CHUNKS) == 0 and tokens.shape[2] % 128 == 0:
        return fused(n, tokens, cotangent, w_first, w_second, mask_first, mask_second, gate_values)
    return plain(tokens, cotangent, w_first, w_second, mask_first, mask_second, gate_values)


def solution(mesh):
    in_specs = (
        P(("groups", "seq"), None, None),
        P("groups", "seq", None),
        P("seq", None),
        P("seq", None),
        P(),
        P(),
        P(("groups", "seq"), None),
    )
    out_specs = (
        P(("groups", "seq"), None, None),
        P(("groups", "seq"), None),
        P(("groups", "seq"), None),
    )
    return jax.shard_map(
        functools.partial(per_device, mesh.shape["seq"]), mesh=mesh, in_specs=in_specs, out_specs=out_specs, check_vma=False
    )
```

```python
import functools
import math

import jax
import jax.numpy as jnp
from jax import lax
from jax.experimental import pallas as pl
from jax.experimental.pallas import tpu as pltpu
from jax.sharding import PartitionSpec as P

BLK = 128
PLANE = 4
CHUNKS = 8
AHEAD = 4
ORDER = (8, 1, 4, 9, 2, 12, 10, 3, 5, 11, 6, 13, 14, 7, 15)
MESH = pl.DeviceIdType.MESH
F32 = jnp.float32
BF16 = jnp.bfloat16


def flip(x, d):
    y = x
    for b in range(d.bit_length()):
        if (d >> b) & 1:
            y = y + (1 << b) - lax.rem(lax.div(x, 1 << b), 2) * (2 << b)
    return y


def drain(ref, sem):
    pltpu.make_async_copy(ref, ref, sem).wait()


def dot(a, b):
    return lax.dot_general(a, b, (((1,), (0,)), ((), ())), preferred_element_type=F32)


def dot_t(a, b):
    return lax.dot_general(a, b, (((1,), (1,)), ((), ())), preferred_element_type=F32)


def mixer_kernel(
    n, tok, cot, w1, w2, mask1, mask2, gate,
    gt_out, g1_out, g2_out, mix_send, mix_recv, back_send, back_recv,
    full1, full2, w_part, part_send, mix_last, result, w1m, w1t, w2t, gate_t, cot_t, stage, tall, tok_in, back_in, out_stage, hidden_b,
    raw1, raw1_in, raw1_plane, raw1_last, raw1_pair, raw2, raw2_in, raw2_plane, raw2_last, raw2_pair,
    gather_s, gather_r, mix_s, mix_r, back_s, back_r, load_sem, stage_sem, out_sem, back_sem,
    sum1_s, sum1_r, sum2_s, sum2_r, last_s, last_r, own_sem, sum3_s, sum3_r,
):
    rows, extent, channels = tok.shape
    planes = n // PLANE
    h = rows // CHUNKS
    wide = n * h
    me = lax.axis_index("seq")
    z, l = lax.div(me, PLANE), lax.rem(me, PLANE)
    factor = 1.0 / math.sqrt(extent * channels)
    lane_chunks = channels // 128
    half_c = min(256, channels)
    whole = CHUNKS - 2
    along_z = tuple(d for d in ORDER if d % PLANE == 0)

    def device(q):
        return {"seq": q}

    def load_tok(c, slot):
        return pltpu.make_async_copy(tok.at[pl.ds(c * h, h)], tok_in.at[slot], load_sem.at[slot])

    def load_cot(c, slot):
        return pltpu.make_async_copy(cot.at[pl.ds(c * wide, wide)], stage.at[slot], stage_sem.at[slot])

    load_tok(0, 0).start()
    load_cot(0, 0).start()

    barrier = pltpu.get_barrier_semaphore()
    for d in range(1, n):
        pl.semaphore_signal(barrier, 1, device_id=device(flip(me, d)), device_id_type=MESH)
    pl.semaphore_wait(barrier, n - 1)

    for a, (w, full) in enumerate(((w1, full1), (w2, full2))):
        for d in range(1, planes):
            pltpu.make_async_remote_copy(
                w, full.at[pl.ds(me * rows, rows)], gather_s.at[a, 0], gather_r.at[a, 0],
                device_id=device(flip(z, d) * PLANE + l), device_id_type=MESH,
            ).start()
    full1[pl.ds(me * rows, rows)] = w1[...]
    full2[pl.ds(me * rows, rows)] = w2[...]

    def spread(a, full):
        drain(full.at[pl.ds(0, (planes - 1) * rows)], gather_r.at[a, 0])
        for d in range(1, PLANE):
            for zz in range(planes):
                part = full.at[pl.ds((zz * PLANE + l) * rows, rows)]
                pltpu.make_async_remote_copy(
                    part, part, gather_s.at[a, 1], gather_r.at[a, 1],
                    device_id=device(z * PLANE + flip(l, d)), device_id_type=MESH,
                ).start()

    def gathered(a, full):
        drain(full.at[pl.ds(0, planes * (PLANE - 1) * rows)], gather_r.at[a, 1])

    def masked(full, mask, out, turn):
        for i in range(extent // BLK):
            for j in range(extent // BLK):
                block = full[i * BLK:(i + 1) * BLK, j * BLK:(j + 1) * BLK].astype(F32)
                block = block * mask[i, j].astype(F32)
                if turn:
                    out[j * BLK:(j + 1) * BLK, i * BLK:(i + 1) * BLK] = block.T.astype(BF16)
                else:
                    out[i * BLK:(i + 1) * BLK, j * BLK:(j + 1) * BLK] = block.astype(BF16)

    gate_t[...] = gate[...].astype(F32).T

    def gate_column(i):
        lanes = lax.broadcasted_iota(jnp.int32, (extent, rows), 1)
        return jnp.sum(jnp.where(lanes == i, gate_t[...], 0.0), axis=1, keepdims=True)

    spread(0, full1)

    for zz in range(planes):
        row0 = pl.multiple_of((zz * PLANE + l) * rows, rows)
        block_row = lax.div(row0, BLK)
        for j in range(extent // BLK):
            js = slice(j * BLK, (j + 1) * BLK)
            block = full1[pl.ds(row0, rows), js].astype(F32) * mask1[block_row, j].astype(F32)
            w_part[zz * rows:(zz + 1) * rows, js] = block.astype(BF16)
    load_tok(0, 0).wait()
    load_tok(1, 1).start()
    lanes_t = lax.broadcasted_iota(jnp.int32, (rows, rows), 1)

    def first_row(t, carry):
        hidden = dot(w_part[...], tok_in[0, t])
        for zz in range(planes):
            cols = pl.ds(pl.multiple_of((zz * PLANE + l) * rows, rows), rows)
            g = jnp.sum(jnp.where(lanes_t == t, gate_t[cols, :], 0.0), axis=1, keepdims=True)
            x = tok_in[0, t, cols, :].astype(F32)
            part_send[zz, t] = (hidden[zz * rows:(zz + 1) * rows] * (x * g)).astype(BF16)
        return carry

    lax.fori_loop(0, h, first_row, 0)
    for d in along_z:
        other = flip(z, d // PLANE)
        pltpu.make_async_remote_copy(
            part_send.at[other], mix_recv.at[0, pl.ds(me * h, h)],
            mix_s.at[0], mix_r.at[0], device_id=device(flip(me, d)), device_id_type=MESH,
        ).start()
    spread(1, full2)
    gathered(0, full1)
    masked(full1, mask1, w1m, False)

    def mix_start(c, order):
        for d in order:
            q = flip(me, d)
            pltpu.make_async_remote_copy(
                mix_send.at[pl.ds(c * h, h), pl.ds(q * rows, rows), :],
                mix_recv.at[c, pl.ds(me * h, h)],
                mix_s.at[c], mix_r.at[c], device_id=device(q), device_id_type=MESH,
            ).start()

    def mix_chunk(c, carry):
        slot = lax.rem(c, 2)

        @pl.when(c > 0)
        def _():
            load_tok(c, slot).wait()

        @pl.when((c > 0) & (c + 1 < CHUNKS))
        def _():
            load_tok(c + 1, 1 - slot).start()

        def row(t, carry):
            g = gate_column(c * h + t)
            for b in range(channels // half_c):
                cs = pl.ds(b * half_c, half_c)
                x = tok_in[slot, t, :, cs]
                hidden = dot(w1m[...], x)
                out_stage[slot, t, :, cs] = (hidden * (x.astype(F32) * g)).astype(BF16)
            return carry

        lax.fori_loop(0, h, row, 0)
        copy = pltpu.make_async_copy(out_stage.at[slot], mix_send.at[pl.ds(c * h, h)], out_sem.at[slot])
        own = pltpu.make_async_copy(
            out_stage.at[slot, :, pl.ds(me * rows, rows), :],
            mix_recv.at[lax.min(c, whole), pl.ds(me * h, h)], own_sem,
        )
        copy.start()
        own.start()
        copy.wait()
        own.wait()

        @pl.when(c == 0)
        def _():
            mix_start(c, tuple(d for d in ORDER if d not in along_z))

        @pl.when((c > 0) & (c < AHEAD))
        def _():
            mix_start(c, ORDER)

        return carry

    lax.fori_loop(0, CHUNKS, mix_chunk, 0)

    gathered(1, full2)
    masked(full1, mask1, w1t, True)
    masked(full2, mask2, w2t, True)
    cot_chunks = extent // wide

    def turn_chunk(c, carry):
        slot = lax.rem(c, 2)
        load_cot(c, slot).wait()

        @pl.when(c + 1 < cot_chunks)
        def _():
            load_cot(c + 1, 1 - slot).start()

        for b in range(lane_chunks):
            cs = pl.ds(b * 128, 128)
            cot_t[:, pl.ds(c * wide, wide), cs] = jnp.swapaxes(stage[slot, :, :, cs], 0, 1)
        return carry

    lax.fori_loop(0, cot_chunks, turn_chunk, 0)

    def back_store(b, s):
        return pltpu.make_async_copy(
            stage.at[s], back_send.at[pl.ds(b * 2 * wide + s * wide, wide)], stage_sem.at[s]
        )

    def back_block(b, carry):
        def column(j, carry):
            tall[j] = dot(w2t[pl.ds(b * 2 * wide, 2 * wide), :], cot_t[j]).astype(BF16)
            return carry

        lax.fori_loop(0, rows, column, 0)
        for s in range(2):
            @pl.when(b > 0)
            def _():
                back_store(b - 1, s).wait()

            for e in range(lane_chunks):
                cs = pl.ds(e * 128, 128)
                stage[s, :, :, cs] = jnp.swapaxes(tall[:, s * wide:(s + 1) * wide, cs], 0, 1)
            back_store(b, s).start()
        return carry

    blocks = extent // (2 * wide)
    lax.fori_loop(0, blocks, back_block, 0)
    for s in range(2):
        back_store(blocks - 1, s).wait()

    def back_start(c, carry):
        for d in ORDER:
            q = flip(me, d)
            pltpu.make_async_remote_copy(
                back_send.at[pl.ds(q * rows + c * h, h)],
                back_recv.at[pl.ds(c * h, h), pl.ds(me * rows, rows), :],
                back_s.at[c], back_r.at[c], device_id=device(q), device_id_type=MESH,
            ).start()
        return carry

    lax.fori_loop(0, CHUNKS, back_start, 0)

    def mix_late(c, carry):
        mix_start(c, ORDER)
        return carry

    lax.fori_loop(AHEAD, whole, mix_late, 0)

    half_rows, half_lanes = rows // 2, channels // 2
    quarters = tuple((a, b) for a in range(2) for b in range(2))

    def last_start(k):
        a, b = quarters[k]
        lanes = pl.ds(b * half_lanes, half_lanes)
        into = mix_last.at[k, pl.ds(me * 2 * h, 2 * h)]
        last_rows = pl.ds(whole * h, 2 * h)
        for d in ORDER:
            q = flip(me, d)
            pltpu.make_async_remote_copy(
                mix_send.at[last_rows, pl.ds(q * rows + a * half_rows, half_rows), lanes], into,
                last_s.at[k], last_r.at[k], device_id=device(q), device_id_type=MESH,
            ).start()
        pltpu.make_async_copy(
            mix_send.at[last_rows, pl.ds(me * rows + a * half_rows, half_rows), lanes], into,
            last_r.at[k],
        ).start()

    last_start(0)
    last_start(1)

    own_in = pltpu.make_async_copy(back_send.at[pl.ds(me * rows, rows)], stage.at[0, pl.ds(0, rows)], own_sem)
    own_in.start()
    own_in.wait()
    own_out = pltpu.make_async_copy(
        stage.at[0, pl.ds(0, rows)], back_recv.at[:, pl.ds(me * rows, rows), :], own_sem
    )
    own_out.start()
    own_out.wait()

    def second(m):
        for s in range(2):
            drain(mix_recv.at[2 * m + s, pl.ds(0, (n - 1) * h)], mix_r.at[2 * m + s])
            copy = pltpu.make_async_copy(mix_recv.at[2 * m + s], stage.at[s], stage_sem.at[s])
            copy.start()
            copy.wait()
            for e in range(lane_chunks):
                cs = pl.ds(e * 128, 128)
                tall[:, s * wide:(s + 1) * wide, cs] = jnp.swapaxes(stage[s, :, :, cs], 0, 1)
        raw2[m] = jnp.zeros(raw2.shape[1:], F32)

        def columns(j, carry):
            part = dot_t(cot_t[4 * j], tall[4 * j])
            for u in range(1, 4):
                part = part + dot_t(cot_t[4 * j + u], tall[4 * j + u])
            raw2[m] += part.reshape(raw2.shape[1:])
            return carry

        lax.fori_loop(0, rows // 4, columns, 0)

    def second_last(m):
        raw2[m] = jnp.zeros(raw2.shape[1:], F32)
        for k, (a, b) in enumerate(quarters):
            drain(mix_last.at[k, pl.ds(0, (n - 1) * 2 * h)], last_s.at[k])
            if k + 2 < len(quarters):
                last_start(k + 2)
            drain(mix_last.at[k], last_r.at[k])
            for e in range(half_lanes // 128):
                tall[a * half_rows:(a + 1) * half_rows, :, pl.ds(b * half_lanes + e * 128, 128)] = (
                    jnp.swapaxes(mix_last[k, :, :, pl.ds(e * 128, 128)], 0, 1)
                )
            lanes = pl.ds(b * half_lanes, half_lanes)

            def columns(j, carry):
                i = a * half_rows + 4 * j
                part = dot_t(cot_t[i, :, lanes], tall[i, :, lanes])
                for u in range(1, 4):
                    part = part + dot_t(cot_t[i + u, :, lanes], tall[i + u, :, lanes])
                raw2[m] += part.reshape(raw2.shape[1:])
                return carry

            lax.fori_loop(0, half_rows // 4, columns, 0)

    def plane_start(k, src, dst):
        for d in range(1, PLANE):
            other = flip(l, d)
            pltpu.make_async_remote_copy(
                src.at[:, other], dst.at[l], sum1_s.at[k], sum1_r.at[k],
                device_id=device(z * PLANE + other), device_id_type=MESH,
            ).start()

    def plane_sum(k, src, dst, total, last):
        drain(dst.at[pl.ds(0, PLANE - 1)], sum1_r.at[k])
        value = src[:, l]
        for d in range(1, PLANE):
            value = value + dst[flip(l, d)]
        total[...] = value
        for u in range(planes // 2):
            other = 2 * u + 1 - lax.rem(z, 2)
            pltpu.make_async_remote_copy(
                total.at[other], last.at[u], sum2_s.at[k], sum2_r.at[k],
                device_id=device(flip(z, 1) * PLANE + l), device_id_type=MESH,
            ).start()

    def pair_sum(k, total, last, pair):
        drain(last.at[pl.ds(0, planes // 2)], sum2_r.at[k])
        for u in range(planes // 2):
            pair[u] = total[2 * u + lax.rem(z, 2)] + last[u]
        for d in range(1, planes // 2):
            u = flip(lax.div(z, 2), d)
            pltpu.make_async_remote_copy(
                pair.at[u], last.at[planes // 2 + lax.div(z, 2)], sum3_s.at[k], sum3_r.at[k],
                device_id=device(flip(z, 2 * d) * PLANE + l), device_id_type=MESH,
            ).start()

    def whole_sum(k, last, pair):
        drain(last.at[pl.ds(0, planes // 2 - 1)], sum3_r.at[k])
        value = pair[lax.div(z, 2)]
        for d in range(1, planes // 2):
            value = value + last[planes // 2 + flip(lax.div(z, 2), d)]
        return value

    parts = CHUNKS // 2
    early = AHEAD // 2
    for m in range(early):
        second(m)
        plane_start(m, raw2.at[m], raw2_in.at[m])

    raw1[...] = jnp.zeros(raw1.shape, F32)

    def store_rows(c, slot):
        return pltpu.make_async_copy(out_stage.at[slot], gt_out.at[pl.ds(c * h, h)], out_sem.at[slot])

    def rows_chunk(c, carry):
        slot = lax.rem(c, 2)
        load_tok(c, slot).start()
        drain(back_recv.at[pl.ds(c * h, h), pl.ds(0, (n - 1) * rows)], back_r.at[c])
        copy = pltpu.make_async_copy(back_recv.at[pl.ds(c * h, h)], back_in, back_sem)
        copy.start()
        load_tok(c, slot).wait()
        copy.wait()

        @pl.when(c >= 2)
        def _():
            store_rows(c - 2, slot).wait()

        def row(t, carry):
            g = gate_column(c * h + t)
            for b in range(channels // half_c):
                cs = pl.ds(b * half_c, half_c)
                x = tok_in[slot, t, :, cs]
                back = back_in[t, :, cs].astype(F32)
                hidden_b[:, cs] = (back * (x.astype(F32) * g)).astype(BF16)
                hidden = dot(w1m[...], x)
                through = dot(w1t[...], hidden_b[:, cs])
                out_stage[slot, t, :, cs] = (g * back * hidden + through).astype(BF16)
            raw1[...] += dot_t(hidden_b[...], tok_in[slot, t]).reshape(raw1.shape)
            return carry

        lax.fori_loop(0, h, row, 0)
        store_rows(c, slot).start()
        return carry

    lax.fori_loop(0, CHUNKS, rows_chunk, 0)
    k1 = parts
    plane_start(k1, raw1, raw1_in)

    def pair_two(m):
        pair_sum(m, raw2_plane.at[m], raw2_last.at[m], raw2_pair.at[m])

    def plane_two(m):
        plane_sum(m, raw2.at[m], raw2_in.at[m], raw2_plane.at[m], raw2_last.at[m])

    lane = lax.broadcasted_iota(jnp.int32, (2 * wide, extent), 0)
    target = lax.broadcasted_iota(jnp.int32, (2 * wide, extent), 1)

    def place_two(m):
        if m < parts - 1:
            piece = lax.div(lane, wide)
            source = lax.div(lane - piece * wide, h)
            index = source * rows + (2 * m + piece) * h + lax.rem(lane, h)
        else:
            index = lax.div(lane, 2 * h) * rows + 2 * m * h + lax.rem(lane, 2 * h)
        value = whole_sum(m, raw2_last.at[m], raw2_pair.at[m])
        result[...] += lax.dot_general(
            value, (index == target).astype(F32), (((1,), (0,)), ((), ())),
            precision=lax.Precision.HIGHEST, preferred_element_type=F32,
        )

    result[...] = jnp.zeros(result.shape, F32)
    for m in range(early):
        plane_two(m)
    plane_sum(k1, raw1, raw1_in, raw1_plane, raw1_last)
    for m in range(early):
        pair_two(m)
    pair_sum(k1, raw1_plane, raw1_last, raw1_pair)
    for m in range(early, parts - 1):
        second(m)
        plane_start(m, raw2.at[m], raw2_in.at[m])
        plane_two(m)
        pair_two(m)
    store_rows(CHUNKS - 2, CHUNKS % 2).wait()
    store_rows(CHUNKS - 1, (CHUNKS - 1) % 2).wait()
    owner = lax.div(me * rows, BLK)
    first = whole_sum(k1, raw1_last, raw1_pair)
    for j in range(extent // BLK):
        js = slice(j * BLK, (j + 1) * BLK)
        g1_out[:, js] = mask1[owner, j].astype(F32) * first[:, js] * factor
    for m in range(parts - 1):
        place_two(m)
    m = parts - 1
    second_last(m)
    plane_start(m, raw2.at[m], raw2_in.at[m])
    plane_two(m)
    pair_two(m)
    place_two(m)
    for j in range(extent // BLK):
        js = slice(j * BLK, (j + 1) * BLK)
        g2_out[:, js] = mask2[owner, j].astype(F32) * result[:, js] * factor

    for a, full in enumerate((full1, full2)):
        drain(full.at[pl.ds(0, (planes - 1) * rows)], gather_s.at[a, 0])
        drain(full.at[pl.ds(0, planes * (PLANE - 1) * rows)], gather_s.at[a, 1])

    def sent(c, carry):
        drain(mix_recv.at[0, pl.ds(0, (n - 1) * h)], back_s.at[c])

        @pl.when(c < whole)
        def _():
            drain(mix_recv.at[0, pl.ds(0, (n - 1) * h)], mix_s.at[c])

        return carry

    lax.fori_loop(0, CHUNKS, sent, 0)
    for m in range(parts):
        drain(raw2_in.at[m, pl.ds(0, PLANE - 1)], sum1_s.at[m])
        drain(raw2_last.at[m, pl.ds(0, planes // 2)], sum2_s.at[m])
        drain(raw2_last.at[m, pl.ds(0, planes // 2 - 1)], sum3_s.at[m])
    drain(raw1_in.at[pl.ds(0, PLANE - 1)], sum1_s.at[k1])
    drain(raw1_last.at[pl.ds(0, planes // 2)], sum2_s.at[k1])
    drain(raw1_last.at[pl.ds(0, planes // 2 - 1)], sum3_s.at[k1])


def fused(n, tokens, cotangent, w_first, w_second, mask_first, mask_second, gate_values):
    rows, extent, channels = tokens.shape
    planes = n // PLANE
    h = rows // CHUNKS
    wide = n * h
    parts = CHUNKS // 2
    hbm = pl.BlockSpec(memory_space=pltpu.HBM)
    vmem = pl.BlockSpec(memory_space=pltpu.VMEM)
    smem = pl.BlockSpec(memory_space=pltpu.SMEM)
    square = pltpu.VMEM((extent, extent), BF16)
    outs = pl.pallas_call(
        functools.partial(mixer_kernel, n),
        out_shape=[
            jax.ShapeDtypeStruct(tokens.shape, BF16),
            jax.ShapeDtypeStruct((rows, extent), F32),
            jax.ShapeDtypeStruct((rows, extent), F32),
            jax.ShapeDtypeStruct((rows, extent, channels), BF16),
            jax.ShapeDtypeStruct((CHUNKS - 1, wide, rows, channels), BF16),
            jax.ShapeDtypeStruct((extent, rows, channels), BF16),
            jax.ShapeDtypeStruct((rows, extent, channels), BF16),
        ],
        in_specs=[hbm, hbm, vmem, vmem, smem, smem, vmem],
        out_specs=[hbm, vmem, vmem, hbm, hbm, hbm, hbm],
        scratch_shapes=[
            square, square,
            pltpu.VMEM((planes * rows, extent), BF16),
            pltpu.VMEM((planes, h, rows, channels), BF16),
            pltpu.VMEM((4, 2 * wide, rows // 2, channels // 2), BF16),
            pltpu.VMEM((rows, extent), F32),
            square, square, square,
            pltpu.VMEM((extent, rows), F32),
            pltpu.VMEM((rows, extent, channels), BF16),
            pltpu.VMEM((2, wide, rows, channels), BF16),
            pltpu.VMEM((rows, 2 * wide, channels), BF16),
            pltpu.VMEM((2, h, extent, channels), BF16),
            pltpu.VMEM((h, extent, channels), BF16),
            pltpu.VMEM((2, h, extent, channels), BF16),
            pltpu.VMEM((extent, channels), BF16),
            pltpu.VMEM((planes, PLANE, rows, extent), F32),
            pltpu.VMEM((PLANE, planes, rows, extent), F32),
            pltpu.VMEM((planes, rows, extent), F32),
            pltpu.VMEM((planes, rows, extent), F32),
            pltpu.VMEM((planes // 2, rows, extent), F32),
            pltpu.VMEM((parts, planes, PLANE, rows, 2 * wide), F32),
            pltpu.VMEM((parts, PLANE, planes, rows, 2 * wide), F32),
            pltpu.VMEM((parts, planes, rows, 2 * wide), F32),
            pltpu.VMEM((parts, planes, rows, 2 * wide), F32),
            pltpu.VMEM((parts, planes // 2, rows, 2 * wide), F32),
            pltpu.SemaphoreType.DMA((2, 2)),
            pltpu.SemaphoreType.DMA((2, 2)),
            pltpu.SemaphoreType.DMA((CHUNKS,)),
            pltpu.SemaphoreType.DMA((CHUNKS,)),
            pltpu.SemaphoreType.DMA((CHUNKS,)),
            pltpu.SemaphoreType.DMA((CHUNKS,)),
            pltpu.SemaphoreType.DMA((2,)),
            pltpu.SemaphoreType.DMA((2,)),
            pltpu.SemaphoreType.DMA((2,)),
            pltpu.SemaphoreType.DMA,
            pltpu.SemaphoreType.DMA((parts + 1,)),
            pltpu.SemaphoreType.DMA((parts + 1,)),
            pltpu.SemaphoreType.DMA((parts + 1,)),
            pltpu.SemaphoreType.DMA((parts + 1,)),
            pltpu.SemaphoreType.DMA((4,)),
            pltpu.SemaphoreType.DMA((4,)),
            pltpu.SemaphoreType.DMA,
            pltpu.SemaphoreType.DMA((parts + 1,)),
            pltpu.SemaphoreType.DMA((parts + 1,)),
        ],
        compiler_params=pltpu.CompilerParams(
            collective_id=0, has_side_effects=True, vmem_limit_bytes=60 * 2**20
        ),
        cost_estimate=pl.CostEstimate(
            flops=12 * rows * extent * extent * channels,
            bytes_accessed=20 * rows * extent * channels,
            transcendentals=0,
        ),
        name="mixer_backward",
    )(tokens, cotangent, w_first, w_second, mask_first, mask_second, gate_values)
    return finish(outs[0], outs[1], outs[2])


def finish_kernel(gt, g1, g2, gt_out, g1_out, g2_out, held, in_sem, out_sem):
    g1_out[...] = g1[...]
    g2_out[...] = g2[...]
    count = in_sem.shape[0]
    step = gt.shape[0] // count
    loads = []
    stores = []
    for k in range(count):
        rows = pl.ds(k * step, step)
        loads.append(pltpu.make_async_copy(gt.at[rows], held.at[rows], in_sem.at[k]))
        stores.append(pltpu.make_async_copy(held.at[rows], gt_out.at[rows], out_sem.at[k]))
    for load in loads:
        load.start()
    for load, store in zip(loads, stores):
        load.wait()
        store.start()
    for store in stores:
        store.wait()


def finish(gt, g1, g2):
    hbm = pl.BlockSpec(memory_space=pltpu.HBM)
    vmem = pl.BlockSpec(memory_space=pltpu.VMEM)
    return pl.pallas_call(
        finish_kernel,
        out_shape=[jax.ShapeDtypeStruct(a.shape, a.dtype) for a in (gt, g1, g2)],
        in_specs=[hbm, vmem, vmem],
        out_specs=[hbm, vmem, vmem],
        scratch_shapes=[
            pltpu.VMEM(gt.shape, gt.dtype),
            pltpu.SemaphoreType.DMA((8,)),
            pltpu.SemaphoreType.DMA((8,)),
        ],
        compiler_params=pltpu.CompilerParams(vmem_limit_bytes=60 * 2**20),
        name="place_outputs",
    )(gt, g1, g2)


def expand_rows(mask, row_ids, extent):
    labels = jnp.arange(mask.shape[0], dtype=jnp.int32)
    row_pick = ((row_ids // BLK)[:, None] == labels[None, :]).astype(jnp.float32)
    col_pick = ((jnp.arange(extent, dtype=jnp.int32) // BLK)[:, None] == labels[None, :]).astype(
        jnp.float32
    )
    return jnp.dot(jnp.dot(row_pick, mask.astype(jnp.float32)), col_pick.T)


def plain(tokens, cotangent, w_first, w_second, mask_first, mask_second, gate_values):
    position = lax.axis_index("seq")
    extent = tokens.shape[1]
    channels = tokens.shape[2]
    shard_rows = w_first.shape[0]
    row_ids = position * shard_rows + jnp.arange(shard_rows, dtype=jnp.int32)
    keep_first = expand_rows(mask_first, row_ids, extent)
    keep_second = expand_rows(mask_second, row_ids, extent)
    local_first = (w_first.astype(jnp.float32) * keep_first).astype(jnp.bfloat16)
    local_second = (w_second.astype(jnp.float32) * keep_second).astype(jnp.bfloat16)
    full = lax.all_gather(jnp.stack([local_first, local_second]), "seq", axis=1, tiled=True)
    full_first, full_second = full[0], full[1]
    shards = extent // shard_rows
    rows = tokens.shape[0]
    cols = cotangent.shape[1]
    flat_cot = lax.optimization_barrier(cotangent.reshape(extent, cols * channels))
    back_flat = lax.dot_general(
        full_second, flat_cot, (((0,), (0,)), ((), ())), preferred_element_type=jnp.float32
    ).astype(jnp.bfloat16)
    back_send = lax.optimization_barrier(back_flat.reshape(shards, rows, cols * channels))
    back_recv = lax.all_to_all(back_send, "seq", split_axis=0, concat_axis=0, tiled=True)
    tokens_late, back_send = lax.optimization_barrier((tokens, back_send))
    gate_full = gate_values.astype(jnp.float32)[:, :, None]
    gated = tokens_late.astype(jnp.float32) * gate_full
    hidden = jnp.einsum("ijc,kj->ikc", tokens_late, full_first, preferred_element_type=jnp.float32)
    mixed = (hidden * gated).astype(jnp.bfloat16)
    mixed_send = mixed.reshape(rows, shards, cols * channels).transpose(1, 0, 2)
    mixed_send, back_recv = lax.optimization_barrier((mixed_send, back_recv))
    flat_cols = lax.all_to_all(mixed_send, "seq", split_axis=0, concat_axis=0, tiled=True)
    back_rows = (
        back_recv.reshape(shards, rows, cols, channels).transpose(1, 0, 2, 3).reshape(tokens.shape)
    )
    back_float = back_rows.astype(jnp.float32)
    back_hidden = (back_float * gated).astype(jnp.bfloat16)
    direct = gate_full * back_float * hidden
    through = jnp.einsum("ikc,kj->ijc", back_hidden, full_first, preferred_element_type=jnp.float32)
    grad_tokens = (direct + through).astype(jnp.bfloat16)
    part_first = jnp.einsum(
        "ikc,ijc->kj", back_hidden, tokens_late, preferred_element_type=jnp.float32
    )
    summed_first = lax.psum_scatter(part_first, "seq", scatter_dimension=0, tiled=True)
    flat_cols, grad_tokens, summed_first = lax.optimization_barrier(
        (flat_cols, grad_tokens, summed_first)
    )
    part_second = lax.dot_general(
        flat_cot,
        flat_cols.reshape(extent, cols * channels),
        (((1,), (1,)), ((), ())),
        preferred_element_type=jnp.float32,
    )
    spread = lax.all_to_all(
        part_second.reshape(shards, shard_rows, extent), "seq", split_axis=0, concat_axis=0, tiled=True
    )
    summed_second = jnp.sum(spread, axis=0)
    factor = 1.0 / math.sqrt(extent * channels)
    grad_first = keep_first * summed_first * factor
    grad_second = keep_second * summed_second * factor
    return (grad_tokens, grad_first, grad_second)


def per_device(n, tokens, cotangent, w_first, w_second, mask_first, mask_second, gate_values):
    if n == 16 and tokens.shape[0] % (4 * CHUNKS) == 0 and tokens.shape[2] % 256 == 0:
        return fused(n, tokens, cotangent, w_first, w_second, mask_first, mask_second, gate_values)
    return plain(tokens, cotangent, w_first, w_second, mask_first, mask_second, gate_values)


def solution(mesh):
    in_specs = (
        P(("groups", "seq"), None, None),
        P("groups", "seq", None),
        P("seq", None),
        P("seq", None),
        P(),
        P(),
        P(("groups", "seq"), None),
    )
    out_specs = (
        P(("groups", "seq"), None, None),
        P(("groups", "seq"), None),
        P(("groups", "seq"), None),
    )
    return jax.shard_map(
        functools.partial(per_device, mesh.shape["seq"]), mesh=mesh, in_specs=in_specs, out_specs=out_specs, check_vma=False
    )
```

```python
import functools
import math

import jax
import jax.numpy as jnp
from jax import lax
from jax.experimental import pallas as pl
from jax.experimental.pallas import tpu as pltpu
from jax.sharding import PartitionSpec as P

BLK = 128
PLANE = 4
CHUNKS = 8
AHEAD = 4
SPLIT = 2
ORDER = (8, 1, 4, 9, 2, 12, 10, 3, 5, 11, 6, 13, 14, 7, 15)
MESH = pl.DeviceIdType.MESH
F32 = jnp.float32
BF16 = jnp.bfloat16


def flip(x, d):
    y = x
    for b in range(d.bit_length()):
        if (d >> b) & 1:
            y = y + (1 << b) - lax.rem(lax.div(x, 1 << b), 2) * (2 << b)
    return y


def drain(ref, sem):
    pltpu.make_async_copy(ref, ref, sem).wait()


def dot(a, b):
    return lax.dot_general(a, b, (((1,), (0,)), ((), ())), preferred_element_type=F32)


def dot_t(a, b):
    return lax.dot_general(a, b, (((1,), (1,)), ((), ())), preferred_element_type=F32)


def mixer_kernel(
    n, tok, cot, w1, w2, mask1, mask2, gate,
    gt_out, g1_out, g2_out, mix_send, mix_recv, back_send, back_recv, mix_last,
    full1, full2, w_part, part_send, result, w1m, w1t, w2t, gate_t, cot_t, stage, tall, tok_in, back_in, out_stage, hidden_b,
    raw1, raw1_in, raw1_plane, raw1_last, raw1_pair, raw2, raw2_in, raw2_plane, raw2_last, raw2_pair,
    gather_s, gather_r, mix_s, mix_r, back_s, back_r, load_sem, stage_sem, out_sem, back_sem,
    sum1_s, sum1_r, sum2_s, sum2_r, last_s, last_r, own_sem, sum3_s, sum3_r,
):
    rows, extent, channels = tok.shape
    planes = n // PLANE
    h = rows // CHUNKS
    wide = n * h
    me = lax.axis_index("seq")
    z, l = lax.div(me, PLANE), lax.rem(me, PLANE)
    factor = 1.0 / math.sqrt(extent * channels)
    lane_chunks = channels // 128
    half_c = min(256, channels)
    whole = CHUNKS - 2
    fine = h // SPLIT
    along_z = tuple(d for d in ORDER if d % PLANE == 0)

    def device(q):
        return {"seq": q}

    def load_tok(c, slot):
        return pltpu.make_async_copy(tok.at[pl.ds(c * h, h)], tok_in.at[slot], load_sem.at[slot])

    def load_cot(c, slot):
        return pltpu.make_async_copy(cot.at[pl.ds(c * wide, wide)], stage.at[slot], stage_sem.at[slot])

    load_tok(0, 0).start()
    load_cot(0, 0).start()

    barrier = pltpu.get_barrier_semaphore()
    for d in range(1, n):
        pl.semaphore_signal(barrier, 1, device_id=device(flip(me, d)), device_id_type=MESH)
    pl.semaphore_wait(barrier, n - 1)

    for a, (w, full) in enumerate(((w1, full1), (w2, full2))):
        for d in range(1, planes):
            pltpu.make_async_remote_copy(
                w, full.at[pl.ds(me * rows, rows)], gather_s.at[a, 0], gather_r.at[a, 0],
                device_id=device(flip(z, d) * PLANE + l), device_id_type=MESH,
            ).start()
    full1[pl.ds(me * rows, rows)] = w1[...]
    full2[pl.ds(me * rows, rows)] = w2[...]

    def spread(a, full):
        drain(full.at[pl.ds(0, (planes - 1) * rows)], gather_r.at[a, 0])
        for d in range(1, PLANE):
            for zz in range(planes):
                part = full.at[pl.ds((zz * PLANE + l) * rows, rows)]
                pltpu.make_async_remote_copy(
                    part, part, gather_s.at[a, 1], gather_r.at[a, 1],
                    device_id=device(z * PLANE + flip(l, d)), device_id_type=MESH,
                ).start()

    def gathered(a, full):
        drain(full.at[pl.ds(0, planes * (PLANE - 1) * rows)], gather_r.at[a, 1])

    def masked(full, mask, out, turn):
        for i in range(extent // BLK):
            for j in range(extent // BLK):
                block = full[i * BLK:(i + 1) * BLK, j * BLK:(j + 1) * BLK].astype(F32)
                block = block * mask[i, j].astype(F32)
                if turn:
                    out[j * BLK:(j + 1) * BLK, i * BLK:(i + 1) * BLK] = block.T.astype(BF16)
                else:
                    out[i * BLK:(i + 1) * BLK, j * BLK:(j + 1) * BLK] = block.astype(BF16)

    gate_t[...] = gate[...].astype(F32).T

    def gate_column(i):
        lanes = lax.broadcasted_iota(jnp.int32, (extent, rows), 1)
        return jnp.sum(jnp.where(lanes == i, gate_t[...], 0.0), axis=1, keepdims=True)

    spread(0, full1)

    for zz in range(planes):
        row0 = pl.multiple_of((zz * PLANE + l) * rows, rows)
        block_row = lax.div(row0, BLK)
        for j in range(extent // BLK):
            js = slice(j * BLK, (j + 1) * BLK)
            block = full1[pl.ds(row0, rows), js].astype(F32) * mask1[block_row, j].astype(F32)
            w_part[zz * rows:(zz + 1) * rows, js] = block.astype(BF16)
    load_tok(0, 0).wait()
    load_tok(1, 1).start()
    lanes_t = lax.broadcasted_iota(jnp.int32, (rows, rows), 1)

    def first_row(t, carry):
        hidden = dot(w_part[...], tok_in[0, t])
        for zz in range(planes):
            cols = pl.ds(pl.multiple_of((zz * PLANE + l) * rows, rows), rows)
            g = jnp.sum(jnp.where(lanes_t == t, gate_t[cols, :], 0.0), axis=1, keepdims=True)
            x = tok_in[0, t, cols, :].astype(F32)
            part_send[zz, t] = (hidden[zz * rows:(zz + 1) * rows] * (x * g)).astype(BF16)
        return carry

    lax.fori_loop(0, h, first_row, 0)
    for d in along_z:
        other = flip(z, d // PLANE)
        pltpu.make_async_remote_copy(
            part_send.at[other], mix_recv.at[0, pl.ds(me * h, h)],
            mix_s.at[0], mix_r.at[0], device_id=device(flip(me, d)), device_id_type=MESH,
        ).start()
    spread(1, full2)
    gathered(0, full1)
    masked(full1, mask1, w1m, False)

    def mix_start(c, order):
        for u in range(SPLIT):
            for d in order:
                q = flip(me, d)
                pltpu.make_async_remote_copy(
                    mix_send.at[pl.ds(c * h + u * fine, fine), pl.ds(q * rows, rows), :],
                    mix_recv.at[c, pl.ds(me * h + u * fine, fine)],
                    mix_s.at[c], mix_r.at[c], device_id=device(q), device_id_type=MESH,
                ).start()

    def mix_chunk(c, carry):
        slot = lax.rem(c, 2)

        @pl.when(c > 0)
        def _():
            load_tok(c, slot).wait()

        @pl.when((c > 0) & (c + 1 < CHUNKS))
        def _():
            load_tok(c + 1, 1 - slot).start()

        def row(t, carry):
            g = gate_column(c * h + t)
            for b in range(channels // half_c):
                cs = pl.ds(b * half_c, half_c)
                x = tok_in[slot, t, :, cs]
                hidden = dot(w1m[...], x)
                out_stage[t, :, cs] = (hidden * (x.astype(F32) * g)).astype(BF16)
            return carry

        lax.fori_loop(0, h, row, 0)
        copy = pltpu.make_async_copy(out_stage, mix_send.at[pl.ds(c * h, h)], out_sem)
        own = pltpu.make_async_copy(
            out_stage.at[:, pl.ds(me * rows, rows), :],
            mix_recv.at[lax.min(c, whole), pl.ds(me * h, h)], own_sem,
        )
        copy.start()
        own.start()
        copy.wait()
        own.wait()

        @pl.when(c == 0)
        def _():
            mix_start(c, tuple(d for d in ORDER if d not in along_z))

        @pl.when((c > 0) & (c < AHEAD))
        def _():
            mix_start(c, ORDER)

        return carry

    lax.fori_loop(0, CHUNKS, mix_chunk, 0)

    gathered(1, full2)
    masked(full1, mask1, w1t, True)
    masked(full2, mask2, w2t, True)
    cot_chunks = extent // wide

    def turn_chunk(c, carry):
        slot = lax.rem(c, 2)
        load_cot(c, slot).wait()

        @pl.when(c + 1 < cot_chunks)
        def _():
            load_cot(c + 1, 1 - slot).start()

        for b in range(lane_chunks):
            cs = pl.ds(b * 128, 128)
            cot_t[:, pl.ds(c * wide, wide), cs] = jnp.swapaxes(stage[slot, :, :, cs], 0, 1)
        return carry

    lax.fori_loop(0, cot_chunks, turn_chunk, 0)

    def back_store(b, s):
        return pltpu.make_async_copy(
            stage.at[s], back_send.at[pl.ds(b * 2 * wide + s * wide, wide)], stage_sem.at[s]
        )

    def back_block(b, carry):
        def column(j, carry):
            tall[j] = dot(w2t[pl.ds(b * 2 * wide, 2 * wide), :], cot_t[j]).astype(BF16)
            return carry

        lax.fori_loop(0, rows, column, 0)
        for s in range(2):
            @pl.when(b > 0)
            def _():
                back_store(b - 1, s).wait()

            for e in range(lane_chunks):
                cs = pl.ds(e * 128, 128)
                stage[s, :, :, cs] = jnp.swapaxes(tall[:, s * wide:(s + 1) * wide, cs], 0, 1)
            back_store(b, s).start()
        return carry

    blocks = extent // (2 * wide)
    lax.fori_loop(0, blocks, back_block, 0)
    for s in range(2):
        back_store(blocks - 1, s).wait()

    def back_start(c, carry):
        for u in range(SPLIT):
            for d in ORDER:
                q = flip(me, d)
                pltpu.make_async_remote_copy(
                    back_send.at[pl.ds(q * rows + c * h + u * fine, fine)],
                    back_recv.at[pl.ds(c * h + u * fine, fine), pl.ds(me * rows, rows), :],
                    back_s.at[c], back_r.at[c], device_id=device(q), device_id_type=MESH,
                ).start()
        return carry

    lax.fori_loop(0, CHUNKS, back_start, 0)

    def mix_late(c, carry):
        mix_start(c, ORDER)
        return carry

    lax.fori_loop(AHEAD, whole, mix_late, 0)

    half_rows, half_lanes = rows // 2, channels // 2
    quarters = tuple((a, b) for a in range(2) for b in range(2))

    def last_start(k):
        a, b = quarters[k]
        lanes = pl.ds(b * half_lanes, half_lanes)
        into = mix_last.at[k, pl.ds(me * 2 * h, 2 * h)]
        last_rows = pl.ds(whole * h, 2 * h)
        for d in ORDER:
            q = flip(me, d)
            pltpu.make_async_remote_copy(
                mix_send.at[last_rows, pl.ds(q * rows + a * half_rows, half_rows), lanes], into,
                last_s.at[k], last_r.at[k], device_id=device(q), device_id_type=MESH,
            ).start()

    def own_last(k):
        a, b = quarters[k]
        lanes = pl.ds(b * half_lanes, half_lanes)
        into = mix_last.at[k, pl.ds(me * 2 * h, 2 * h)]
        cols = pl.ds(me * rows + a * half_rows, half_rows)
        held = stage.at[0, pl.ds(0, 2 * h), pl.ds(0, half_rows), pl.ds(0, half_lanes)]
        load = pltpu.make_async_copy(mix_send.at[pl.ds(whole * h, 2 * h), cols, lanes], held, own_sem)
        load.start()
        load.wait()
        store = pltpu.make_async_copy(held, into, own_sem)
        store.start()
        store.wait()

    last_start(0)
    last_start(1)
    for k in range(len(quarters)):
        own_last(k)

    own_in = pltpu.make_async_copy(back_send.at[pl.ds(me * rows, rows)], stage.at[0, pl.ds(0, rows)], own_sem)
    own_in.start()
    own_in.wait()
    own_out = pltpu.make_async_copy(
        stage.at[0, pl.ds(0, rows)], back_recv.at[:, pl.ds(me * rows, rows), :], own_sem
    )
    own_out.start()
    own_out.wait()

    def second(m):
        for s in range(2):
            drain(mix_recv.at[2 * m + s, pl.ds(0, (n - 1) * h)], mix_r.at[2 * m + s])
            copy = pltpu.make_async_copy(mix_recv.at[2 * m + s], stage.at[s], stage_sem.at[s])
            copy.start()
            copy.wait()
            for e in range(lane_chunks):
                cs = pl.ds(e * 128, 128)
                tall[:, s * wide:(s + 1) * wide, cs] = jnp.swapaxes(stage[s, :, :, cs], 0, 1)
        raw2[m] = jnp.zeros(raw2.shape[1:], F32)

        def columns(j, carry):
            part = dot_t(cot_t[4 * j], tall[4 * j])
            for u in range(1, 4):
                part = part + dot_t(cot_t[4 * j + u], tall[4 * j + u])
            raw2[m] += part.reshape(raw2.shape[1:])
            return carry

        lax.fori_loop(0, rows // 4, columns, 0)

    def second_last(m):
        raw2[m] = jnp.zeros(raw2.shape[1:], F32)
        for k, (a, b) in enumerate(quarters):
            drain(mix_last.at[k, pl.ds(0, (n - 1) * 2 * h)], last_s.at[k])
            if k + 2 < len(quarters):
                last_start(k + 2)
            drain(mix_last.at[k, pl.ds(0, (n - 1) * 2 * h)], last_r.at[k])
            loads = [
                pltpu.make_async_copy(
                    mix_last.at[k, pl.ds(s * wide, wide)],
                    stage.at[s, :, pl.ds(0, half_rows), pl.ds(0, half_lanes)], stage_sem.at[s],
                )
                for s in range(2)
            ]
            for load in loads:
                load.start()
            for s in range(2):
                loads[s].wait()
                for e in range(half_lanes // 128):
                    cs = pl.ds(b * half_lanes + e * 128, 128)
                    tall[a * half_rows:(a + 1) * half_rows, s * wide:(s + 1) * wide, cs] = jnp.swapaxes(
                        stage[s, :, 0:half_rows, pl.ds(e * 128, 128)], 0, 1
                    )
            lanes = pl.ds(b * half_lanes, half_lanes)

            def columns(j, carry):
                i = a * half_rows + 4 * j
                part = dot_t(cot_t[i, :, lanes], tall[i, :, lanes])
                for u in range(1, 4):
                    part = part + dot_t(cot_t[i + u, :, lanes], tall[i + u, :, lanes])
                raw2[m] += part.reshape(raw2.shape[1:])
                return carry

            lax.fori_loop(0, half_rows // 4, columns, 0)

    def plane_start(k, src, dst):
        for d in range(1, PLANE):
            other = flip(l, d)
            pltpu.make_async_remote_copy(
                src.at[:, other], dst.at[l], sum1_s.at[k], sum1_r.at[k],
                device_id=device(z * PLANE + other), device_id_type=MESH,
            ).start()

    def plane_sum(k, src, dst, total, last):
        drain(dst.at[pl.ds(0, PLANE - 1)], sum1_r.at[k])
        value = src[:, l]
        for d in range(1, PLANE):
            value = value + dst[flip(l, d)]
        total[...] = value
        for u in range(planes // 2):
            other = 2 * u + 1 - lax.rem(z, 2)
            pltpu.make_async_remote_copy(
                total.at[other], last.at[u], sum2_s.at[k], sum2_r.at[k],
                device_id=device(flip(z, 1) * PLANE + l), device_id_type=MESH,
            ).start()

    def pair_sum(k, total, last, pair):
        drain(last.at[pl.ds(0, planes // 2)], sum2_r.at[k])
        for u in range(planes // 2):
            pair[u] = total[2 * u + lax.rem(z, 2)] + last[u]
        for d in range(1, planes // 2):
            u = flip(lax.div(z, 2), d)
            pltpu.make_async_remote_copy(
                pair.at[u], last.at[planes // 2 + lax.div(z, 2)], sum3_s.at[k], sum3_r.at[k],
                device_id=device(flip(z, 2 * d) * PLANE + l), device_id_type=MESH,
            ).start()

    def whole_sum(k, last, pair):
        drain(last.at[pl.ds(0, planes // 2 - 1)], sum3_r.at[k])
        value = pair[lax.div(z, 2)]
        for d in range(1, planes // 2):
            value = value + last[planes // 2 + flip(lax.div(z, 2), d)]
        return value

    parts = CHUNKS // 2
    early = AHEAD // 2
    for m in range(early):
        second(m)
        plane_start(m, raw2.at[m], raw2_in.at[m])

    raw1[...] = jnp.zeros(raw1.shape, F32)

    def rows_chunk(c, carry):
        slot = lax.rem(c, 2)
        load_tok(c, slot).start()
        drain(back_recv.at[pl.ds(c * h, h), pl.ds(0, (n - 1) * rows)], back_r.at[c])
        copy = pltpu.make_async_copy(back_recv.at[pl.ds(c * h, h)], back_in, back_sem)
        copy.start()
        load_tok(c, slot).wait()
        copy.wait()

        def row(t, carry):
            g = gate_column(c * h + t)
            for b in range(channels // half_c):
                cs = pl.ds(b * half_c, half_c)
                x = tok_in[slot, t, :, cs]
                back = back_in[t, :, cs].astype(F32)
                hidden_b[:, cs] = (back * (x.astype(F32) * g)).astype(BF16)
                hidden = dot(w1m[...], x)
                through = dot(w1t[...], hidden_b[:, cs])
                gt_out[c * h + t, :, cs] = (g * back * hidden + through).astype(BF16)
            raw1[...] += dot_t(hidden_b[...], tok_in[slot, t]).reshape(raw1.shape)
            return carry

        lax.fori_loop(0, h, row, 0)
        return carry

    lax.fori_loop(0, CHUNKS, rows_chunk, 0)
    k1 = parts
    plane_start(k1, raw1, raw1_in)

    def pair_two(m):
        pair_sum(m, raw2_plane.at[m], raw2_last.at[m], raw2_pair.at[m])

    def plane_two(m):
        plane_sum(m, raw2.at[m], raw2_in.at[m], raw2_plane.at[m], raw2_last.at[m])

    lane = lax.broadcasted_iota(jnp.int32, (2 * wide, extent), 0)
    target = lax.broadcasted_iota(jnp.int32, (2 * wide, extent), 1)

    def place_two(m):
        if m < parts - 1:
            piece = lax.div(lane, wide)
            source = lax.div(lane - piece * wide, h)
            index = source * rows + (2 * m + piece) * h + lax.rem(lane, h)
        else:
            index = lax.div(lane, 2 * h) * rows + 2 * m * h + lax.rem(lane, 2 * h)
        value = whole_sum(m, raw2_last.at[m], raw2_pair.at[m])
        result[...] += lax.dot_general(
            value, (index == target).astype(F32), (((1,), (0,)), ((), ())),
            precision=lax.Precision.HIGHEST, preferred_element_type=F32,
        )

    result[...] = jnp.zeros(result.shape, F32)
    for m in range(early):
        plane_two(m)
    plane_sum(k1, raw1, raw1_in, raw1_plane, raw1_last)
    for m in range(early):
        pair_two(m)
    pair_sum(k1, raw1_plane, raw1_last, raw1_pair)
    for m in range(early, parts - 1):
        second(m)
        plane_start(m, raw2.at[m], raw2_in.at[m])
        plane_two(m)
        pair_two(m)
    owner = lax.div(me * rows, BLK)
    first = whole_sum(k1, raw1_last, raw1_pair)
    for j in range(extent // BLK):
        js = slice(j * BLK, (j + 1) * BLK)
        g1_out[:, js] = mask1[owner, j].astype(F32) * first[:, js] * factor
    for m in range(parts - 1):
        place_two(m)
    m = parts - 1
    second_last(m)
    plane_start(m, raw2.at[m], raw2_in.at[m])
    plane_two(m)
    pair_two(m)
    place_two(m)
    for j in range(extent // BLK):
        js = slice(j * BLK, (j + 1) * BLK)
        g2_out[:, js] = mask2[owner, j].astype(F32) * result[:, js] * factor

    for a, full in enumerate((full1, full2)):
        drain(full.at[pl.ds(0, (planes - 1) * rows)], gather_s.at[a, 0])
        drain(full.at[pl.ds(0, planes * (PLANE - 1) * rows)], gather_s.at[a, 1])

    def sent(c, carry):
        drain(mix_recv.at[0, pl.ds(0, (n - 1) * h)], back_s.at[c])

        @pl.when(c < whole)
        def _():
            drain(mix_recv.at[0, pl.ds(0, (n - 1) * h)], mix_s.at[c])

        return carry

    lax.fori_loop(0, CHUNKS, sent, 0)
    for m in range(parts):
        drain(raw2_in.at[m, pl.ds(0, PLANE - 1)], sum1_s.at[m])
        drain(raw2_last.at[m, pl.ds(0, planes // 2)], sum2_s.at[m])
        drain(raw2_last.at[m, pl.ds(0, planes // 2 - 1)], sum3_s.at[m])
    drain(raw1_in.at[pl.ds(0, PLANE - 1)], sum1_s.at[k1])
    drain(raw1_last.at[pl.ds(0, planes // 2)], sum2_s.at[k1])
    drain(raw1_last.at[pl.ds(0, planes // 2 - 1)], sum3_s.at[k1])


def fused(n, tokens, cotangent, w_first, w_second, mask_first, mask_second, gate_values):
    rows, extent, channels = tokens.shape
    planes = n // PLANE
    h = rows // CHUNKS
    wide = n * h
    parts = CHUNKS // 2
    hbm = pl.BlockSpec(memory_space=pltpu.HBM)
    vmem = pl.BlockSpec(memory_space=pltpu.VMEM)
    smem = pl.BlockSpec(memory_space=pltpu.SMEM)
    square = pltpu.VMEM((extent, extent), BF16)
    outs = pl.pallas_call(
        functools.partial(mixer_kernel, n),
        out_shape=[
            pltpu.VMEM(tokens.shape, BF16),
            pltpu.VMEM((rows, extent), F32),
            pltpu.VMEM((rows, extent), F32),
            jax.ShapeDtypeStruct((rows, extent, channels), BF16),
            jax.ShapeDtypeStruct((CHUNKS - 1, wide, rows, channels), BF16),
            jax.ShapeDtypeStruct((extent, rows, channels), BF16),
            jax.ShapeDtypeStruct((rows, extent, channels), BF16),
            jax.ShapeDtypeStruct((4, 2 * wide, rows // 2, channels // 2), BF16),
        ],
        in_specs=[hbm, hbm, vmem, vmem, smem, smem, vmem],
        out_specs=[vmem, vmem, vmem, hbm, hbm, hbm, hbm, hbm],
        scratch_shapes=[
            square, square,
            pltpu.VMEM((planes * rows, extent), BF16),
            pltpu.VMEM((planes, h, rows, channels), BF16),
            pltpu.VMEM((rows, extent), F32),
            square, square, square,
            pltpu.VMEM((extent, rows), F32),
            pltpu.VMEM((rows, extent, channels), BF16),
            pltpu.VMEM((2, wide, rows, channels), BF16),
            pltpu.VMEM((rows, 2 * wide, channels), BF16),
            pltpu.VMEM((2, h, extent, channels), BF16),
            pltpu.VMEM((h, extent, channels), BF16),
            pltpu.VMEM((h, extent, channels), BF16),
            pltpu.VMEM((extent, channels), BF16),
            pltpu.VMEM((planes, PLANE, rows, extent), F32),
            pltpu.VMEM((PLANE, planes, rows, extent), F32),
            pltpu.VMEM((planes, rows, extent), F32),
            pltpu.VMEM((planes, rows, extent), F32),
            pltpu.VMEM((planes // 2, rows, extent), F32),
            pltpu.VMEM((parts, planes, PLANE, rows, 2 * wide), F32),
            pltpu.VMEM((parts, PLANE, planes, rows, 2 * wide), F32),
            pltpu.VMEM((parts, planes, rows, 2 * wide), F32),
            pltpu.VMEM((parts, planes, rows, 2 * wide), F32),
            pltpu.VMEM((parts, planes // 2, rows, 2 * wide), F32),
            pltpu.SemaphoreType.DMA((2, 2)),
            pltpu.SemaphoreType.DMA((2, 2)),
            pltpu.SemaphoreType.DMA((CHUNKS,)),
            pltpu.SemaphoreType.DMA((CHUNKS,)),
            pltpu.SemaphoreType.DMA((CHUNKS,)),
            pltpu.SemaphoreType.DMA((CHUNKS,)),
            pltpu.SemaphoreType.DMA((2,)),
            pltpu.SemaphoreType.DMA((2,)),
            pltpu.SemaphoreType.DMA,
            pltpu.SemaphoreType.DMA,
            pltpu.SemaphoreType.DMA((parts + 1,)),
            pltpu.SemaphoreType.DMA((parts + 1,)),
            pltpu.SemaphoreType.DMA((parts + 1,)),
            pltpu.SemaphoreType.DMA((parts + 1,)),
            pltpu.SemaphoreType.DMA((4,)),
            pltpu.SemaphoreType.DMA((4,)),
            pltpu.SemaphoreType.DMA,
            pltpu.SemaphoreType.DMA((parts + 1,)),
            pltpu.SemaphoreType.DMA((parts + 1,)),
        ],
        compiler_params=pltpu.CompilerParams(
            collective_id=0, has_side_effects=True, vmem_limit_bytes=46 * 2**20
        ),
        cost_estimate=pl.CostEstimate(
            flops=12 * rows * extent * extent * channels,
            bytes_accessed=20 * rows * extent * channels,
            transcendentals=0,
        ),
        name="mixer_backward",
    )(tokens, cotangent, w_first, w_second, mask_first, mask_second, gate_values)
    return tuple(outs[:3])


def expand_rows(mask, row_ids, extent):
    labels = jnp.arange(mask.shape[0], dtype=jnp.int32)
    row_pick = ((row_ids // BLK)[:, None] == labels[None, :]).astype(jnp.float32)
    col_pick = ((jnp.arange(extent, dtype=jnp.int32) // BLK)[:, None] == labels[None, :]).astype(
        jnp.float32
    )
    return jnp.dot(jnp.dot(row_pick, mask.astype(jnp.float32)), col_pick.T)


def plain(tokens, cotangent, w_first, w_second, mask_first, mask_second, gate_values):
    position = lax.axis_index("seq")
    extent = tokens.shape[1]
    channels = tokens.shape[2]
    shard_rows = w_first.shape[0]
    row_ids = position * shard_rows + jnp.arange(shard_rows, dtype=jnp.int32)
    keep_first = expand_rows(mask_first, row_ids, extent)
    keep_second = expand_rows(mask_second, row_ids, extent)
    local_first = (w_first.astype(jnp.float32) * keep_first).astype(jnp.bfloat16)
    local_second = (w_second.astype(jnp.float32) * keep_second).astype(jnp.bfloat16)
    full = lax.all_gather(jnp.stack([local_first, local_second]), "seq", axis=1, tiled=True)
    full_first, full_second = full[0], full[1]
    shards = extent // shard_rows
    rows = tokens.shape[0]
    cols = cotangent.shape[1]
    flat_cot = lax.optimization_barrier(cotangent.reshape(extent, cols * channels))
    back_flat = lax.dot_general(
        full_second, flat_cot, (((0,), (0,)), ((), ())), preferred_element_type=jnp.float32
    ).astype(jnp.bfloat16)
    back_send = lax.optimization_barrier(back_flat.reshape(shards, rows, cols * channels))
    back_recv = lax.all_to_all(back_send, "seq", split_axis=0, concat_axis=0, tiled=True)
    tokens_late, back_send = lax.optimization_barrier((tokens, back_send))
    gate_full = gate_values.astype(jnp.float32)[:, :, None]
    gated = tokens_late.astype(jnp.float32) * gate_full
    hidden = jnp.einsum("ijc,kj->ikc", tokens_late, full_first, preferred_element_type=jnp.float32)
    mixed = (hidden * gated).astype(jnp.bfloat16)
    mixed_send = mixed.reshape(rows, shards, cols * channels).transpose(1, 0, 2)
    mixed_send, back_recv = lax.optimization_barrier((mixed_send, back_recv))
    flat_cols = lax.all_to_all(mixed_send, "seq", split_axis=0, concat_axis=0, tiled=True)
    back_rows = (
        back_recv.reshape(shards, rows, cols, channels).transpose(1, 0, 2, 3).reshape(tokens.shape)
    )
    back_float = back_rows.astype(jnp.float32)
    back_hidden = (back_float * gated).astype(jnp.bfloat16)
    direct = gate_full * back_float * hidden
    through = jnp.einsum("ikc,kj->ijc", back_hidden, full_first, preferred_element_type=jnp.float32)
    grad_tokens = (direct + through).astype(jnp.bfloat16)
    part_first = jnp.einsum(
        "ikc,ijc->kj", back_hidden, tokens_late, preferred_element_type=jnp.float32
    )
    summed_first = lax.psum_scatter(part_first, "seq", scatter_dimension=0, tiled=True)
    flat_cols, grad_tokens, summed_first = lax.optimization_barrier(
        (flat_cols, grad_tokens, summed_first)
    )
    part_second = lax.dot_general(
        flat_cot,
        flat_cols.reshape(extent, cols * channels),
        (((1,), (1,)), ((), ())),
        preferred_element_type=jnp.float32,
    )
    spread = lax.all_to_all(
        part_second.reshape(shards, shard_rows, extent), "seq", split_axis=0, concat_axis=0, tiled=True
    )
    summed_second = jnp.sum(spread, axis=0)
    factor = 1.0 / math.sqrt(extent * channels)
    grad_first = keep_first * summed_first * factor
    grad_second = keep_second * summed_second * factor
    return (grad_tokens, grad_first, grad_second)


def per_device(n, tokens, cotangent, w_first, w_second, mask_first, mask_second, gate_values):
    if n == 16 and tokens.shape[0] % (4 * CHUNKS) == 0 and tokens.shape[2] % 256 == 0:
        return fused(n, tokens, cotangent, w_first, w_second, mask_first, mask_second, gate_values)
    return plain(tokens, cotangent, w_first, w_second, mask_first, mask_second, gate_values)


def solution(mesh):
    in_specs = (
        P(("groups", "seq"), None, None),
        P("groups", "seq", None),
        P("seq", None),
        P("seq", None),
        P(),
        P(),
        P(("groups", "seq"), None),
    )
    out_specs = (
        P(("groups", "seq"), None, None),
        P(("groups", "seq"), None),
        P(("groups", "seq"), None),
    )
    return jax.shard_map(
        functools.partial(per_device, mesh.shape["seq"]), mesh=mesh, in_specs=in_specs, out_specs=out_specs, check_vma=False
    )
```

```python
import functools
import math

import jax
import jax.numpy as jnp
from jax import lax
from jax.experimental import pallas as pl
from jax.experimental.pallas import tpu as pltpu
from jax.sharding import PartitionSpec as P

BLK = 128
PLANE = 4
CHUNKS = 8
AHEAD = 4
SPLIT = 2
ORDER = (8, 1, 4, 9, 2, 12, 10, 3, 5, 11, 6, 13, 14, 7, 15)
MESH = pl.DeviceIdType.MESH
F32 = jnp.float32
BF16 = jnp.bfloat16


def flip(x, d):
    y = x
    for b in range(d.bit_length()):
        if (d >> b) & 1:
            y = y + (1 << b) - lax.rem(lax.div(x, 1 << b), 2) * (2 << b)
    return y


def drain(ref, sem):
    pltpu.make_async_copy(ref, ref, sem).wait()


def dot(a, b):
    return lax.dot_general(a, b, (((1,), (0,)), ((), ())), preferred_element_type=F32)


def dot_t(a, b):
    return lax.dot_general(a, b, (((1,), (1,)), ((), ())), preferred_element_type=F32)


def mixer_kernel(
    n, tok, cot, w1, w2, mask1, mask2, gate,
    gt_out, g1_out, g2_out, mix_send, mix_recv, back_send, back_recv, mix_last,
    full1, full2, w_part, part_send, result, w1m, w1t, w2t, gate_t, cot_t, stage, tall, tok_in, back_in, out_stage, hidden_b,
    raw1, raw1_in, raw1_plane, raw1_last, raw1_pair, raw2, raw2_in, raw2_plane, raw2_last, raw2_pair,
    gather_s, gather_r, mix_s, mix_r, back_s, back_r, load_sem, stage_sem, out_sem, back_sem,
    sum1_s, sum1_r, sum2_s, sum2_r, last_s, last_r, own_sem, sum3_s, sum3_r,
):
    rows, extent, channels = tok.shape
    planes = n // PLANE
    h = rows // CHUNKS
    wide = n * h
    me = lax.axis_index("seq")
    z, l = lax.div(me, PLANE), lax.rem(me, PLANE)
    factor = 1.0 / math.sqrt(extent * channels)
    lane_chunks = channels // 128
    half_c = min(256, channels)
    whole = CHUNKS - 2
    fine = h // SPLIT
    along_z = tuple(d for d in ORDER if d % PLANE == 0)

    def device(q):
        return {"seq": q}

    def load_tok(c, slot):
        return pltpu.make_async_copy(tok.at[pl.ds(c * h, h)], tok_in.at[slot], load_sem.at[slot])

    def load_cot(c, slot):
        return pltpu.make_async_copy(cot.at[pl.ds(c * wide, wide)], stage.at[slot], stage_sem.at[slot])

    load_tok(0, 0).start()
    load_cot(0, 0).start()

    barrier = pltpu.get_barrier_semaphore()
    for d in range(1, n):
        pl.semaphore_signal(barrier, 1, device_id=device(flip(me, d)), device_id_type=MESH)
    pl.semaphore_wait(barrier, n - 1)

    for a, (w, full) in enumerate(((w1, full1), (w2, full2))):
        for d in range(1, planes):
            pltpu.make_async_remote_copy(
                w, full.at[pl.ds(me * rows, rows)], gather_s.at[a, 0], gather_r.at[a, 0],
                device_id=device(flip(z, d) * PLANE + l), device_id_type=MESH,
            ).start()
    full1[pl.ds(me * rows, rows)] = w1[...]
    full2[pl.ds(me * rows, rows)] = w2[...]

    def spread(a, full):
        drain(full.at[pl.ds(0, (planes - 1) * rows)], gather_r.at[a, 0])
        for d in range(1, PLANE):
            for zz in range(planes):
                part = full.at[pl.ds((zz * PLANE + l) * rows, rows)]
                pltpu.make_async_remote_copy(
                    part, part, gather_s.at[a, 1], gather_r.at[a, 1],
                    device_id=device(z * PLANE + flip(l, d)), device_id_type=MESH,
                ).start()

    def gathered(a, full):
        drain(full.at[pl.ds(0, planes * (PLANE - 1) * rows)], gather_r.at[a, 1])

    def masked(full, mask, out, turn):
        for i in range(extent // BLK):
            for j in range(extent // BLK):
                block = full[i * BLK:(i + 1) * BLK, j * BLK:(j + 1) * BLK].astype(F32)
                block = block * mask[i, j].astype(F32)
                if turn:
                    out[j * BLK:(j + 1) * BLK, i * BLK:(i + 1) * BLK] = block.T.astype(BF16)
                else:
                    out[i * BLK:(i + 1) * BLK, j * BLK:(j + 1) * BLK] = block.astype(BF16)

    gate_t[...] = gate[...].astype(F32).T

    def gate_column(i):
        lanes = lax.broadcasted_iota(jnp.int32, (extent, rows), 1)
        return jnp.sum(jnp.where(lanes == i, gate_t[...], 0.0), axis=1, keepdims=True)

    spread(0, full1)

    for zz in range(planes):
        row0 = pl.multiple_of((zz * PLANE + l) * rows, rows)
        block_row = lax.div(row0, BLK)
        for j in range(extent // BLK):
            js = slice(j * BLK, (j + 1) * BLK)
            block = full1[pl.ds(row0, rows), js].astype(F32) * mask1[block_row, j].astype(F32)
            w_part[zz * rows:(zz + 1) * rows, js] = block.astype(BF16)
    load_tok(0, 0).wait()
    load_tok(1, 1).start()
    lanes_t = lax.broadcasted_iota(jnp.int32, (rows, rows), 1)

    def first_row(t, carry):
        hidden = dot(w_part[...], tok_in[0, t])
        for zz in range(planes):
            cols = pl.ds(pl.multiple_of((zz * PLANE + l) * rows, rows), rows)
            g = jnp.sum(jnp.where(lanes_t == t, gate_t[cols, :], 0.0), axis=1, keepdims=True)
            x = tok_in[0, t, cols, :].astype(F32)
            part_send[zz, t] = (hidden[zz * rows:(zz + 1) * rows] * (x * g)).astype(BF16)
        for d in along_z:
            other = flip(z, d // PLANE)
            pltpu.make_async_remote_copy(
                part_send.at[other, pl.ds(t, 1)], mix_recv.at[0, pl.ds(me * h + t, 1)],
                mix_s.at[0], mix_r.at[0], device_id=device(flip(me, d)), device_id_type=MESH,
            ).start()
        return carry

    lax.fori_loop(0, h, first_row, 0)
    spread(1, full2)
    gathered(0, full1)
    masked(full1, mask1, w1m, False)

    def mix_start(c, order):
        for u in range(SPLIT):
            for d in order:
                q = flip(me, d)
                pltpu.make_async_remote_copy(
                    mix_send.at[pl.ds(c * h + u * fine, fine), pl.ds(q * rows, rows), :],
                    mix_recv.at[c, pl.ds(me * h + u * fine, fine)],
                    mix_s.at[c], mix_r.at[c], device_id=device(q), device_id_type=MESH,
                ).start()

    def mix_chunk(c, carry):
        slot = lax.rem(c, 2)

        @pl.when(c > 0)
        def _():
            load_tok(c, slot).wait()

        @pl.when((c > 0) & (c + 1 < CHUNKS))
        def _():
            load_tok(c + 1, 1 - slot).start()

        def row(t, carry):
            g = gate_column(c * h + t)
            for b in range(channels // half_c):
                cs = pl.ds(b * half_c, half_c)
                x = tok_in[slot, t, :, cs]
                hidden = dot(w1m[...], x)
                out_stage[t, :, cs] = (hidden * (x.astype(F32) * g)).astype(BF16)
            return carry

        lax.fori_loop(0, h, row, 0)
        copy = pltpu.make_async_copy(out_stage, mix_send.at[pl.ds(c * h, h)], out_sem)
        own = pltpu.make_async_copy(
            out_stage.at[:, pl.ds(me * rows, rows), :],
            mix_recv.at[lax.min(c, whole), pl.ds(me * h, h)], own_sem,
        )
        copy.start()
        own.start()
        copy.wait()
        own.wait()

        @pl.when(c == 0)
        def _():
            mix_start(c, tuple(d for d in ORDER if d not in along_z))

        @pl.when((c > 0) & (c < AHEAD))
        def _():
            mix_start(c, ORDER)

        return carry

    lax.fori_loop(0, CHUNKS, mix_chunk, 0)

    gathered(1, full2)
    masked(full1, mask1, w1t, True)
    masked(full2, mask2, w2t, True)
    cot_chunks = extent // wide

    def turn_chunk(c, carry):
        slot = lax.rem(c, 2)
        load_cot(c, slot).wait()

        @pl.when(c + 1 < cot_chunks)
        def _():
            load_cot(c + 1, 1 - slot).start()

        for b in range(lane_chunks):
            cs = pl.ds(b * 128, 128)
            cot_t[:, pl.ds(c * wide, wide), cs] = jnp.swapaxes(stage[slot, :, :, cs], 0, 1)
        return carry

    lax.fori_loop(0, cot_chunks, turn_chunk, 0)

    def back_store(b, s):
        return pltpu.make_async_copy(
            stage.at[s], back_send.at[pl.ds(b * 2 * wide + s * wide, wide)], stage_sem.at[s]
        )

    def back_block(b, carry):
        def column(j, carry):
            tall[j] = dot(w2t[pl.ds(b * 2 * wide, 2 * wide), :], cot_t[j]).astype(BF16)
            return carry

        lax.fori_loop(0, rows, column, 0)
        for s in range(2):
            @pl.when(b > 0)
            def _():
                back_store(b - 1, s).wait()

            for e in range(lane_chunks):
                cs = pl.ds(e * 128, 128)
                stage[s, :, :, cs] = jnp.swapaxes(tall[:, s * wide:(s + 1) * wide, cs], 0, 1)
            back_store(b, s).start()
        return carry

    blocks = extent // (2 * wide)
    lax.fori_loop(0, blocks, back_block, 0)
    for s in range(2):
        back_store(blocks - 1, s).wait()

    def back_start(c, carry):
        for u in range(SPLIT):
            for d in ORDER:
                q = flip(me, d)
                pltpu.make_async_remote_copy(
                    back_send.at[pl.ds(q * rows + c * h + u * fine, fine)],
                    back_recv.at[pl.ds(c * h + u * fine, fine), pl.ds(me * rows, rows), :],
                    back_s.at[c], back_r.at[c], device_id=device(q), device_id_type=MESH,
                ).start()
        return carry

    lax.fori_loop(0, CHUNKS, back_start, 0)

    def mix_late(c, carry):
        mix_start(c, ORDER)
        return carry

    lax.fori_loop(AHEAD, whole, mix_late, 0)

    half_rows, half_lanes = rows // 2, channels // 2
    quarters = tuple((a, b) for a in range(2) for b in range(2))

    def last_start(k):
        a, b = quarters[k]
        lanes = pl.ds(b * half_lanes, half_lanes)
        into = mix_last.at[k, pl.ds(me * 2 * h, 2 * h)]
        last_rows = pl.ds(whole * h, 2 * h)
        for d in ORDER:
            q = flip(me, d)
            pltpu.make_async_remote_copy(
                mix_send.at[last_rows, pl.ds(q * rows + a * half_rows, half_rows), lanes], into,
                last_s.at[k], last_r.at[k], device_id=device(q), device_id_type=MESH,
            ).start()

    def own_last(k):
        a, b = quarters[k]
        lanes = pl.ds(b * half_lanes, half_lanes)
        into = mix_last.at[k, pl.ds(me * 2 * h, 2 * h)]
        cols = pl.ds(me * rows + a * half_rows, half_rows)
        held = stage.at[0, pl.ds(0, 2 * h), pl.ds(0, half_rows), pl.ds(0, half_lanes)]
        load = pltpu.make_async_copy(mix_send.at[pl.ds(whole * h, 2 * h), cols, lanes], held, own_sem)
        load.start()
        load.wait()
        store = pltpu.make_async_copy(held, into, own_sem)
        store.start()
        store.wait()

    last_start(0)
    last_start(1)
    for k in range(len(quarters)):
        own_last(k)

    own_in = pltpu.make_async_copy(back_send.at[pl.ds(me * rows, rows)], stage.at[0, pl.ds(0, rows)], own_sem)
    own_in.start()
    own_in.wait()
    own_out = pltpu.make_async_copy(
        stage.at[0, pl.ds(0, rows)], back_recv.at[:, pl.ds(me * rows, rows), :], own_sem
    )
    own_out.start()
    own_out.wait()

    def second(m):
        for s in range(2):
            drain(mix_recv.at[2 * m + s, pl.ds(0, (n - 1) * h)], mix_r.at[2 * m + s])
            copy = pltpu.make_async_copy(mix_recv.at[2 * m + s], stage.at[s], stage_sem.at[s])
            copy.start()
            copy.wait()
            for e in range(lane_chunks):
                cs = pl.ds(e * 128, 128)
                tall[:, s * wide:(s + 1) * wide, cs] = jnp.swapaxes(stage[s, :, :, cs], 0, 1)
        raw2[m] = jnp.zeros(raw2.shape[1:], F32)

        def columns(j, carry):
            part = dot_t(cot_t[4 * j], tall[4 * j])
            for u in range(1, 4):
                part = part + dot_t(cot_t[4 * j + u], tall[4 * j + u])
            raw2[m] += part.reshape(raw2.shape[1:])
            return carry

        lax.fori_loop(0, rows // 4, columns, 0)

    def second_last(m):
        raw2[m] = jnp.zeros(raw2.shape[1:], F32)
        for k, (a, b) in enumerate(quarters):
            drain(mix_last.at[k, pl.ds(0, (n - 1) * 2 * h)], last_s.at[k])
            if k + 2 < len(quarters):
                last_start(k + 2)
            drain(mix_last.at[k, pl.ds(0, (n - 1) * 2 * h)], last_r.at[k])
            loads = [
                pltpu.make_async_copy(
                    mix_last.at[k, pl.ds(s * wide, wide)],
                    stage.at[s, :, pl.ds(0, half_rows), pl.ds(0, half_lanes)], stage_sem.at[s],
                )
                for s in range(2)
            ]
            for load in loads:
                load.start()
            for s in range(2):
                loads[s].wait()
                for e in range(half_lanes // 128):
                    cs = pl.ds(b * half_lanes + e * 128, 128)
                    tall[a * half_rows:(a + 1) * half_rows, s * wide:(s + 1) * wide, cs] = jnp.swapaxes(
                        stage[s, :, 0:half_rows, pl.ds(e * 128, 128)], 0, 1
                    )
            lanes = pl.ds(b * half_lanes, half_lanes)

            def columns(j, carry):
                i = a * half_rows + 4 * j
                part = dot_t(cot_t[i, :, lanes], tall[i, :, lanes])
                for u in range(1, 4):
                    part = part + dot_t(cot_t[i + u, :, lanes], tall[i + u, :, lanes])
                raw2[m] += part.reshape(raw2.shape[1:])
                return carry

            lax.fori_loop(0, half_rows // 4, columns, 0)

    def plane_start(k, src, dst):
        for d in range(1, PLANE):
            other = flip(l, d)
            pltpu.make_async_remote_copy(
                src.at[:, other], dst.at[l], sum1_s.at[k], sum1_r.at[k],
                device_id=device(z * PLANE + other), device_id_type=MESH,
            ).start()

    def plane_sum(k, src, dst, total, last):
        drain(dst.at[pl.ds(0, PLANE - 1)], sum1_r.at[k])
        value = src[:, l]
        for d in range(1, PLANE):
            value = value + dst[flip(l, d)]
        total[...] = value
        for u in range(planes // 2):
            other = 2 * u + 1 - lax.rem(z, 2)
            pltpu.make_async_remote_copy(
                total.at[other], last.at[u], sum2_s.at[k], sum2_r.at[k],
                device_id=device(flip(z, 1) * PLANE + l), device_id_type=MESH,
            ).start()

    def direct_sum(k, src, dst, total, last):
        drain(dst.at[pl.ds(0, PLANE - 1)], sum1_r.at[k])
        value = src[:, l]
        for d in range(1, PLANE):
            value = value + dst[flip(l, d)]
        total[...] = value
        for d in range(1, planes):
            other = flip(z, d)
            pltpu.make_async_remote_copy(
                total.at[other], last.at[z], sum2_s.at[k], sum2_r.at[k],
                device_id=device(other * PLANE + l), device_id_type=MESH,
            ).start()

    def direct_whole(k, total, last):
        drain(last.at[pl.ds(0, planes - 1)], sum2_r.at[k])
        value = total[z]
        for d in range(1, planes):
            value = value + last[flip(z, d)]
        return value

    def pair_sum(k, total, last, pair):
        drain(last.at[pl.ds(0, planes // 2)], sum2_r.at[k])
        for u in range(planes // 2):
            pair[u] = total[2 * u + lax.rem(z, 2)] + last[u]
        for d in range(1, planes // 2):
            u = flip(lax.div(z, 2), d)
            pltpu.make_async_remote_copy(
                pair.at[u], last.at[planes // 2 + lax.div(z, 2)], sum3_s.at[k], sum3_r.at[k],
                device_id=device(flip(z, 2 * d) * PLANE + l), device_id_type=MESH,
            ).start()

    def whole_sum(k, last, pair):
        drain(last.at[pl.ds(0, planes // 2 - 1)], sum3_r.at[k])
        value = pair[lax.div(z, 2)]
        for d in range(1, planes // 2):
            value = value + last[planes // 2 + flip(lax.div(z, 2), d)]
        return value

    parts = CHUNKS // 2
    early = AHEAD // 2
    for m in range(early):
        second(m)
        plane_start(m, raw2.at[m], raw2_in.at[m])

    raw1[...] = jnp.zeros(raw1.shape, F32)

    def rows_chunk(c, carry):
        slot = lax.rem(c, 2)
        load_tok(c, slot).start()
        drain(back_recv.at[pl.ds(c * h, h), pl.ds(0, (n - 1) * rows)], back_r.at[c])
        copy = pltpu.make_async_copy(back_recv.at[pl.ds(c * h, h)], back_in, back_sem)
        copy.start()
        load_tok(c, slot).wait()
        copy.wait()

        def row(t, carry):
            g = gate_column(c * h + t)
            for b in range(channels // half_c):
                cs = pl.ds(b * half_c, half_c)
                x = tok_in[slot, t, :, cs]
                back = back_in[t, :, cs].astype(F32)
                hidden_b[:, cs] = (back * (x.astype(F32) * g)).astype(BF16)
                hidden = dot(w1m[...], x)
                through = dot(w1t[...], hidden_b[:, cs])
                gt_out[c * h + t, :, cs] = (g * back * hidden + through).astype(BF16)
            raw1[...] += dot_t(hidden_b[...], tok_in[slot, t]).reshape(raw1.shape)
            return carry

        lax.fori_loop(0, h, row, 0)
        return carry

    lax.fori_loop(0, CHUNKS, rows_chunk, 0)
    k1 = parts
    plane_start(k1, raw1, raw1_in)

    def pair_two(m):
        pair_sum(m, raw2_plane.at[m], raw2_last.at[m], raw2_pair.at[m])

    def plane_two(m):
        plane_sum(m, raw2.at[m], raw2_in.at[m], raw2_plane.at[m], raw2_last.at[m])

    lane = lax.broadcasted_iota(jnp.int32, (2 * wide, extent), 0)
    target = lax.broadcasted_iota(jnp.int32, (2 * wide, extent), 1)

    def place_two(m):
        if m < parts - 1:
            piece = lax.div(lane, wide)
            source = lax.div(lane - piece * wide, h)
            index = source * rows + (2 * m + piece) * h + lax.rem(lane, h)
        else:
            index = lax.div(lane, 2 * h) * rows + 2 * m * h + lax.rem(lane, 2 * h)
        if m < parts - 1:
            value = whole_sum(m, raw2_last.at[m], raw2_pair.at[m])
        else:
            value = direct_whole(m, raw2_plane.at[m], raw2_last.at[m])
        result[...] += lax.dot_general(
            value, (index == target).astype(F32), (((1,), (0,)), ((), ())),
            precision=lax.Precision.HIGHEST, preferred_element_type=F32,
        )

    result[...] = jnp.zeros(result.shape, F32)
    for m in range(early):
        plane_two(m)
    plane_sum(k1, raw1, raw1_in, raw1_plane, raw1_last)
    for m in range(early):
        pair_two(m)
    pair_sum(k1, raw1_plane, raw1_last, raw1_pair)
    for m in range(early, parts - 1):
        second(m)
        plane_start(m, raw2.at[m], raw2_in.at[m])
        plane_two(m)
        pair_two(m)
    owner = lax.div(me * rows, BLK)
    first = whole_sum(k1, raw1_last, raw1_pair)
    for j in range(extent // BLK):
        js = slice(j * BLK, (j + 1) * BLK)
        g1_out[:, js] = mask1[owner, j].astype(F32) * first[:, js] * factor
    for m in range(parts - 1):
        place_two(m)
    m = parts - 1
    second_last(m)
    plane_start(m, raw2.at[m], raw2_in.at[m])
    direct_sum(m, raw2.at[m], raw2_in.at[m], raw2_plane.at[m], raw2_last.at[m])
    place_two(m)
    for j in range(extent // BLK):
        js = slice(j * BLK, (j + 1) * BLK)
        g2_out[:, js] = mask2[owner, j].astype(F32) * result[:, js] * factor

    for a, full in enumerate((full1, full2)):
        drain(full.at[pl.ds(0, (planes - 1) * rows)], gather_s.at[a, 0])
        drain(full.at[pl.ds(0, planes * (PLANE - 1) * rows)], gather_s.at[a, 1])

    def sent(c, carry):
        drain(mix_recv.at[0, pl.ds(0, (n - 1) * h)], back_s.at[c])

        @pl.when(c < whole)
        def _():
            drain(mix_recv.at[0, pl.ds(0, (n - 1) * h)], mix_s.at[c])

        return carry

    lax.fori_loop(0, CHUNKS, sent, 0)
    for m in range(parts):
        drain(raw2_in.at[m, pl.ds(0, PLANE - 1)], sum1_s.at[m])
        if m < parts - 1:
            drain(raw2_last.at[m, pl.ds(0, planes // 2)], sum2_s.at[m])
            drain(raw2_last.at[m, pl.ds(0, planes // 2 - 1)], sum3_s.at[m])
        else:
            drain(raw2_last.at[m, pl.ds(0, planes - 1)], sum2_s.at[m])
    drain(raw1_in.at[pl.ds(0, PLANE - 1)], sum1_s.at[k1])
    drain(raw1_last.at[pl.ds(0, planes // 2)], sum2_s.at[k1])
    drain(raw1_last.at[pl.ds(0, planes // 2 - 1)], sum3_s.at[k1])


def fused(n, tokens, cotangent, w_first, w_second, mask_first, mask_second, gate_values):
    rows, extent, channels = tokens.shape
    planes = n // PLANE
    h = rows // CHUNKS
    wide = n * h
    parts = CHUNKS // 2
    hbm = pl.BlockSpec(memory_space=pltpu.HBM)
    vmem = pl.BlockSpec(memory_space=pltpu.VMEM)
    smem = pl.BlockSpec(memory_space=pltpu.SMEM)
    square = pltpu.VMEM((extent, extent), BF16)
    outs = pl.pallas_call(
        functools.partial(mixer_kernel, n),
        out_shape=[
            pltpu.VMEM(tokens.shape, BF16),
            pltpu.VMEM((rows, extent), F32),
            pltpu.VMEM((rows, extent), F32),
            jax.ShapeDtypeStruct((rows, extent, channels), BF16),
            jax.ShapeDtypeStruct((CHUNKS - 1, wide, rows, channels), BF16),
            jax.ShapeDtypeStruct((extent, rows, channels), BF16),
            jax.ShapeDtypeStruct((rows, extent, channels), BF16),
            jax.ShapeDtypeStruct((4, 2 * wide, rows // 2, channels // 2), BF16),
        ],
        in_specs=[hbm, hbm, vmem, vmem, smem, smem, vmem],
        out_specs=[vmem, vmem, vmem, hbm, hbm, hbm, hbm, hbm],
        scratch_shapes=[
            square, square,
            pltpu.VMEM((planes * rows, extent), BF16),
            pltpu.VMEM((planes, h, rows, channels), BF16),
            pltpu.VMEM((rows, extent), F32),
            square, square, square,
            pltpu.VMEM((extent, rows), F32),
            pltpu.VMEM((rows, extent, channels), BF16),
            pltpu.VMEM((2, wide, rows, channels), BF16),
            pltpu.VMEM((rows, 2 * wide, channels), BF16),
            pltpu.VMEM((2, h, extent, channels), BF16),
            pltpu.VMEM((h, extent, channels), BF16),
            pltpu.VMEM((h, extent, channels), BF16),
            pltpu.VMEM((extent, channels), BF16),
            pltpu.VMEM((planes, PLANE, rows, extent), F32),
            pltpu.VMEM((PLANE, planes, rows, extent), F32),
            pltpu.VMEM((planes, rows, extent), F32),
            pltpu.VMEM((planes, rows, extent), F32),
            pltpu.VMEM((planes // 2, rows, extent), F32),
            pltpu.VMEM((parts, planes, PLANE, rows, 2 * wide), F32),
            pltpu.VMEM((parts, PLANE, planes, rows, 2 * wide), F32),
            pltpu.VMEM((parts, planes, rows, 2 * wide), F32),
            pltpu.VMEM((parts, planes, rows, 2 * wide), F32),
            pltpu.VMEM((parts, planes // 2, rows, 2 * wide), F32),
            pltpu.SemaphoreType.DMA((2, 2)),
            pltpu.SemaphoreType.DMA((2, 2)),
            pltpu.SemaphoreType.DMA((CHUNKS,)),
            pltpu.SemaphoreType.DMA((CHUNKS,)),
            pltpu.SemaphoreType.DMA((CHUNKS,)),
            pltpu.SemaphoreType.DMA((CHUNKS,)),
            pltpu.SemaphoreType.DMA((2,)),
            pltpu.SemaphoreType.DMA((2,)),
            pltpu.SemaphoreType.DMA,
            pltpu.SemaphoreType.DMA,
            pltpu.SemaphoreType.DMA((parts + 1,)),
            pltpu.SemaphoreType.DMA((parts + 1,)),
            pltpu.SemaphoreType.DMA((parts + 1,)),
            pltpu.SemaphoreType.DMA((parts + 1,)),
            pltpu.SemaphoreType.DMA((4,)),
            pltpu.SemaphoreType.DMA((4,)),
            pltpu.SemaphoreType.DMA,
            pltpu.SemaphoreType.DMA((parts + 1,)),
            pltpu.SemaphoreType.DMA((parts + 1,)),
        ],
        compiler_params=pltpu.CompilerParams(
            collective_id=0, has_side_effects=True, vmem_limit_bytes=46 * 2**20
        ),
        cost_estimate=pl.CostEstimate(
            flops=12 * rows * extent * extent * channels,
            bytes_accessed=20 * rows * extent * channels,
            transcendentals=0,
        ),
        name="mixer_backward",
    )(tokens, cotangent, w_first, w_second, mask_first, mask_second, gate_values)
    return tuple(outs[:3])


def expand_rows(mask, row_ids, extent):
    labels = jnp.arange(mask.shape[0], dtype=jnp.int32)
    row_pick = ((row_ids // BLK)[:, None] == labels[None, :]).astype(jnp.float32)
    col_pick = ((jnp.arange(extent, dtype=jnp.int32) // BLK)[:, None] == labels[None, :]).astype(
        jnp.float32
    )
    return jnp.dot(jnp.dot(row_pick, mask.astype(jnp.float32)), col_pick.T)


def plain(tokens, cotangent, w_first, w_second, mask_first, mask_second, gate_values):
    position = lax.axis_index("seq")
    extent = tokens.shape[1]
    channels = tokens.shape[2]
    shard_rows = w_first.shape[0]
    row_ids = position * shard_rows + jnp.arange(shard_rows, dtype=jnp.int32)
    keep_first = expand_rows(mask_first, row_ids, extent)
    keep_second = expand_rows(mask_second, row_ids, extent)
    local_first = (w_first.astype(jnp.float32) * keep_first).astype(jnp.bfloat16)
    local_second = (w_second.astype(jnp.float32) * keep_second).astype(jnp.bfloat16)
    full = lax.all_gather(jnp.stack([local_first, local_second]), "seq", axis=1, tiled=True)
    full_first, full_second = full[0], full[1]
    shards = extent // shard_rows
    rows = tokens.shape[0]
    cols = cotangent.shape[1]
    flat_cot = lax.optimization_barrier(cotangent.reshape(extent, cols * channels))
    back_flat = lax.dot_general(
        full_second, flat_cot, (((0,), (0,)), ((), ())), preferred_element_type=jnp.float32
    ).astype(jnp.bfloat16)
    back_send = lax.optimization_barrier(back_flat.reshape(shards, rows, cols * channels))
    back_recv = lax.all_to_all(back_send, "seq", split_axis=0, concat_axis=0, tiled=True)
    tokens_late, back_send = lax.optimization_barrier((tokens, back_send))
    gate_full = gate_values.astype(jnp.float32)[:, :, None]
    gated = tokens_late.astype(jnp.float32) * gate_full
    hidden = jnp.einsum("ijc,kj->ikc", tokens_late, full_first, preferred_element_type=jnp.float32)
    mixed = (hidden * gated).astype(jnp.bfloat16)
    mixed_send = mixed.reshape(rows, shards, cols * channels).transpose(1, 0, 2)
    mixed_send, back_recv = lax.optimization_barrier((mixed_send, back_recv))
    flat_cols = lax.all_to_all(mixed_send, "seq", split_axis=0, concat_axis=0, tiled=True)
    back_rows = (
        back_recv.reshape(shards, rows, cols, channels).transpose(1, 0, 2, 3).reshape(tokens.shape)
    )
    back_float = back_rows.astype(jnp.float32)
    back_hidden = (back_float * gated).astype(jnp.bfloat16)
    direct = gate_full * back_float * hidden
    through = jnp.einsum("ikc,kj->ijc", back_hidden, full_first, preferred_element_type=jnp.float32)
    grad_tokens = (direct + through).astype(jnp.bfloat16)
    part_first = jnp.einsum(
        "ikc,ijc->kj", back_hidden, tokens_late, preferred_element_type=jnp.float32
    )
    summed_first = lax.psum_scatter(part_first, "seq", scatter_dimension=0, tiled=True)
    flat_cols, grad_tokens, summed_first = lax.optimization_barrier(
        (flat_cols, grad_tokens, summed_first)
    )
    part_second = lax.dot_general(
        flat_cot,
        flat_cols.reshape(extent, cols * channels),
        (((1,), (1,)), ((), ())),
        preferred_element_type=jnp.float32,
    )
    spread = lax.all_to_all(
        part_second.reshape(shards, shard_rows, extent), "seq", split_axis=0, concat_axis=0, tiled=True
    )
    summed_second = jnp.sum(spread, axis=0)
    factor = 1.0 / math.sqrt(extent * channels)
    grad_first = keep_first * summed_first * factor
    grad_second = keep_second * summed_second * factor
    return (grad_tokens, grad_first, grad_second)


def per_device(n, tokens, cotangent, w_first, w_second, mask_first, mask_second, gate_values):
    if n == 16 and tokens.shape[0] % (4 * CHUNKS) == 0 and tokens.shape[2] % 256 == 0:
        return fused(n, tokens, cotangent, w_first, w_second, mask_first, mask_second, gate_values)
    return plain(tokens, cotangent, w_first, w_second, mask_first, mask_second, gate_values)


def solution(mesh):
    in_specs = (
        P(("groups", "seq"), None, None),
        P("groups", "seq", None),
        P("seq", None),
        P("seq", None),
        P(),
        P(),
        P(("groups", "seq"), None),
    )
    out_specs = (
        P(("groups", "seq"), None, None),
        P(("groups", "seq"), None),
        P(("groups", "seq"), None),
    )
    return jax.shard_map(
        functools.partial(per_device, mesh.shape["seq"]), mesh=mesh, in_specs=in_specs, out_specs=out_specs, check_vma=False
    )
```
